32 devices in a mesh: gx: 2 (over y), gy: 4 (over x, core), gz: 4 (over z).
Axes of the slice: x: 2, y: 2, z: 4, core: 2. Of those that a mesh axis runs over, the one named last changes fastest.
Arguments:
- velocity: float32 [3, 64, 128, 512], P(None, 'gx', 'gy', 'gz'), may hold values from -3 to 3
- box_level: float32 [512, 16, 256], P(('gx', 'gy', 'gz')), may hold values from -9 to 9
- corners: int32 [512, 3], P(('gx', 'gy', 'gz')), may hold values from 0 to 112, as said below
- owner_list: int32 [512], P(('gx', 'gy', 'gz')), may hold values from -1 to 15, as said below
Outputs:
- new_velocity: float32 [3, 64, 128, 512], P(None, 'gx', 'gy', 'gz')
- level_sets: float32 [512, 16, 256], P(('gx', 'gy', 'gz'))
- curvature: float32 [512, 16, 256], P(('gx', 'gy', 'gz'))
The draws below stay inside these ranges and needn't reach their ends.
Inputs may be any that keep to these rules, and one draw needn't show every extreme that they name: `owner_list`: -1 marks an empty slot. The live slots of one device name different helpers, numbered in the order of the devices of its gy+gz group (gy slowest) at the device's own index along gx; every helper is named by exactly 8 slots of its group; a device has 0 to 16 live slots, and some device of every group has 16. `corners`: columns 0, 1, 2 lie in 0 to 16, 16, 112: every box lies inside its home device's block. Boxes may intersect.
All inputs are finite; a program needn't handle non-finite values.
Results may differ from the reference program's by a relative error of at most 0.0003.
Values sent between devices are 32-bit elements; how exact they have to be, the bound alone decides.
A program may use at most 128 MiB of HBM per device.

```python
import math
import jax
import jax.numpy as jnp
from jax import lax

CX = 32
CY = 32
CZ = 128
BOX = 16
ITERS = 12
GROUP = 16
HELP = 8
SLOTS = 16
SLOTS_ALL = 512
NX = 64
NY = 128
NZ = 512
N_GY = 4
N_GZ = 4


def draw_corners(key, part):
    along_x = jax.random.randint(jax.random.fold_in(key, 11), (SLOTS_ALL, 1), 0, CX - BOX + 1)
    along_y = jax.random.randint(jax.random.fold_in(key, 13), (SLOTS_ALL, 1), 0, CY - BOX + 1)
    along_z = jax.random.randint(jax.random.fold_in(key, 17), (SLOTS_ALL, 1), 0, CZ - BOX + 1)
    return jnp.concatenate([along_x, along_y, along_z], axis=1).astype(jnp.int32)


def group_owners(group_key):
    pair_count = GROUP // 2
    subkeys = jax.random.split(group_key, 4)
    excess = jax.random.randint(subkeys[0], (pair_count,), 0, HELP + 1)
    excess = excess.at[0].set(HELP)
    counts = jnp.concatenate([HELP + excess, HELP - excess])
    counts = counts[jax.random.permutation(subkeys[1], GROUP)]
    starts = jnp.cumsum(counts) - counts
    relabel = jax.random.permutation(subkeys[2], GROUP).astype(jnp.int32)
    position = jnp.arange(SLOTS, dtype=jnp.int32)
    serial = starts[:, None] + position[None, :]
    named_ids = jnp.where(position[None, :] < counts[:, None], relabel[serial % GROUP], -1)
    home_keys = jax.random.split(subkeys[3], GROUP)
    orders = jax.vmap(lambda home_key: jax.random.permutation(home_key, SLOTS))(home_keys)
    return jnp.take_along_axis(named_ids, orders, axis=1)


def draw_owner_list(key, part):
    group_keys = jax.random.split(jax.random.fold_in(key, 29), SLOTS_ALL // (SLOTS * GROUP))
    owners = jax.vmap(group_owners)(group_keys)
    return owners.reshape(SLOTS_ALL).astype(jnp.int32)


def shard_levels(stream_key, dims, pieces, smallest, largest):
    loudness, own = 1.0, jax.random.fold_in(stream_key, 6)
    for dim, parts in pieces:
        heights = jnp.exp(jax.random.uniform(jax.random.fold_in(own, dim), (parts,), jnp.float32, smallest / len(pieces), largest / len(pieces)))
        loudness = loudness * jnp.repeat(heights, dims[dim] // parts).reshape([-1 if axis == dim else 1 for axis in range(len(dims))])
    return loudness


def centred(own_key, dims, deviation, limit, shards=(), kind=jnp.bfloat16):
    factor_of = shard_levels(own_key, dims, shards, -0.22, 0.18) if shards else 1.0
    array = jax.random.normal(own_key, dims, jnp.float32) * deviation * factor_of
    return jnp.minimum(jnp.maximum(array, -limit), limit).astype(kind)


def setup_inputs(seed: int = 0) -> dict:
    splits = jax.random.split(jax.random.key(seed), 5)
    velocity = centred(splits[0], (3, NX, NY, NZ), 0.5, 3.0, ((1, 2), (2, 4), (3, 4)), jnp.float32)
    box_level = centred(splits[1], (SLOTS_ALL, BOX, BOX * BOX), 1.5, 9.0, ((0, 32),), jnp.float32)
    corners = draw_corners(jax.random.fold_in(splits[4], 71), 0)
    owner_list = draw_owner_list(jax.random.fold_in(splits[4], 71), 0)
    return {"velocity": velocity, "box_level": box_level, "corners": corners, "owner_list": owner_list}


box_step = 0.25
pseudo_step = 0.3
weno_floor = 1e-06
band_width = 1.5
tension = 2.0
grid_step = 0.2
viscosity = 0.1
normal_floor = 0.5

def neighbour(values, across, forward):
    length = values.shape[-2]
    plane_size = values.shape[-1]
    if across == 0:
        if forward:
            return jnp.concatenate([values[..., 1:, :], values[..., -1:, :]], axis=-2)
        return jnp.concatenate([values[..., :1, :], values[..., :-1, :]], axis=-2)
    stride = length if across == 1 else 1
    places = jnp.arange(plane_size, dtype=jnp.int32)
    column = places // length if across == 1 else places % length
    if forward:
        shifted = jnp.concatenate([values[..., stride:], values[..., :stride]], axis=-1)
        return jnp.where(column == length - 1, values, shifted)
    shifted = jnp.concatenate([values[..., plane_size - stride:], values[..., :plane_size - stride]], axis=-1)
    return jnp.where(column == 0, values, shifted)

def weno_blend(slope_one, slope_two, slope_three, slope_four, slope_five):
    smooth_one = 13.0 / 12.0 * (slope_one - 2.0 * slope_two + slope_three) ** 2 + 0.25 * (slope_one - 4.0 * slope_two + 3.0 * slope_three) ** 2
    smooth_two = 13.0 / 12.0 * (slope_two - 2.0 * slope_three + slope_four) ** 2 + 0.25 * (slope_two - slope_four) ** 2
    smooth_three = 13.0 / 12.0 * (slope_three - 2.0 * slope_four + slope_five) ** 2 + 0.25 * (3.0 * slope_three - 4.0 * slope_four + slope_five) ** 2
    weight_one = 0.1 / (weno_floor + smooth_one) ** 2
    weight_two = 0.6 / (weno_floor + smooth_two) ** 2
    weight_three = 0.3 / (weno_floor + smooth_three) ** 2
    poly_one = slope_one / 3.0 - 7.0 * slope_two / 6.0 + 11.0 * slope_three / 6.0
    poly_two = -slope_two / 6.0 + 5.0 * slope_three / 6.0 + slope_four / 3.0
    poly_three = slope_three / 3.0 + 5.0 * slope_four / 6.0 - slope_five / 6.0
    return (weight_one * poly_one + weight_two * poly_two + weight_three * poly_three) / (weight_one + weight_two + weight_three)

def upwind_slopes(values, across):
    behind = values - neighbour(values, across, False)
    back_one = neighbour(behind, across, False)
    back_two = neighbour(back_one, across, False)
    ahead_one = neighbour(behind, across, True)
    ahead_two = neighbour(ahead_one, across, True)
    ahead_three = neighbour(ahead_two, across, True)
    minus_side = weno_blend(back_two, back_one, behind, ahead_one, ahead_two)
    plus_side = weno_blend(ahead_three, ahead_two, ahead_one, behind, back_one)
    return (minus_side, plus_side)

def central_slopes(values):
    return [0.5 * (neighbour(values, across, True) - neighbour(values, across, False)) for across in range(3)]

def evolve_boxes(levels, motion):
    change = jnp.zeros_like(levels)
    for across in range(3):
        minus_side, plus_side = upwind_slopes(levels, across)
        speed_d = motion[:, across]
        change = change + jnp.maximum(speed_d, 0.0) * minus_side + jnp.minimum(speed_d, 0.0) * plus_side
    advected = levels - box_step * change
    sign_soft = advected / jnp.sqrt(advected * advected + 1.0)
    outside = advected > 0.0

    def one_sweep(counter, current):
        squared = jnp.zeros_like(current)
        for across in range(3):
            behind = current - neighbour(current, across, False)
            ahead_d = neighbour(current, across, True) - current
            upper_sq = jnp.maximum(jnp.maximum(behind, 0.0) ** 2, jnp.minimum(ahead_d, 0.0) ** 2)
            lower_sq = jnp.maximum(jnp.minimum(behind, 0.0) ** 2, jnp.maximum(ahead_d, 0.0) ** 2)
            squared = squared + jnp.where(outside, upper_sq, lower_sq)
        return current - pseudo_step * sign_soft * (jnp.sqrt(squared) - 1.0)
    settled = lax.fori_loop(0, ITERS, one_sweep, advected)
    slopes = central_slopes(settled)
    magnitude = jnp.maximum(jnp.sqrt(slopes[0] ** 2 + slopes[1] ** 2 + slopes[2] ** 2), normal_floor)
    bending = jnp.zeros_like(settled)
    for across in range(3):
        unit_d = slopes[across] / magnitude
        bending = bending + 0.5 * (neighbour(unit_d, across, True) - neighbour(unit_d, across, False))
    return (settled, bending)

def surface_force(levels, bending):
    slopes = central_slopes(levels)
    delta_band = jnp.exp(-(levels / band_width) ** 2) / (band_width * math.sqrt(math.pi))
    strength = tension * bending * delta_band
    return jnp.stack([strength * slopes[0], strength * slopes[1], strength * slopes[2]], axis=1)

def tendency(padded):
    centre = padded[:, 1:-1, 1:-1, 1:-1]
    uppers = (padded[:, 2:, 1:-1, 1:-1], padded[:, 1:-1, 2:, 1:-1], padded[:, 1:-1, 1:-1, 2:])
    lowers = (padded[:, :-2, 1:-1, 1:-1], padded[:, 1:-1, :-2, 1:-1], padded[:, 1:-1, 1:-1, :-2])
    advect = jnp.zeros_like(centre)
    spread = -6.0 * centre
    for across in range(3):
        advect = advect + centre[across:across + 1] * (uppers[across] - lowers[across]) * 0.5
        spread = spread + uppers[across] + lowers[across]
    return viscosity * spread - advect

def wrap_pad(values):
    return jnp.pad(values, ((0, 0), (1, 1), (1, 1), (1, 1)), mode='wrap')

def reference(velocity, box_level, corners, owner_list):
    alive_mask = (owner_list >= 0).astype(jnp.float32)
    slot_ids = jnp.arange(SLOTS_ALL, dtype=jnp.int32)
    device = slot_ids // SLOTS
    anchor_x = (device // (N_GY * N_GZ) * CX + corners[:, 0]).astype(jnp.int32)
    anchor_y = (device // N_GZ % N_GY * CY + corners[:, 1]).astype(jnp.int32)
    anchor_z = (device % N_GZ * CZ + corners[:, 2]).astype(jnp.int32)
    nought = jnp.zeros((), jnp.int32)

    def one_box(packed):
        level_box, place_x, place_y, place_z = packed
        motion = lax.dynamic_slice(velocity, (nought, place_x, place_y, place_z), (3, BOX, BOX, BOX))
        motion = motion.reshape(1, 3, BOX, BOX * BOX)
        settled, bending = evolve_boxes(level_box[None], motion)
        return (settled[0], bending[0])
    settled, bending = lax.map(one_box, (box_level, anchor_x, anchor_y, anchor_z))
    settled = settled * alive_mask[:, None, None]
    bending = bending * alive_mask[:, None, None]
    predictor = velocity + grid_step * tendency(wrap_pad(velocity))
    second = predictor + grid_step * tendency(wrap_pad(predictor))
    stepped = 0.5 * (velocity + second)

    def deposit(slot_no, grid_now):
        push_box = surface_force(settled[slot_no][None], bending[slot_no][None])[0].reshape(3, BOX, BOX, BOX)
        corner_at = (nought, anchor_x[slot_no], anchor_y[slot_no], anchor_z[slot_no])
        region = lax.dynamic_slice(grid_now, corner_at, (3, BOX, BOX, BOX))
        return lax.dynamic_update_slice(grid_now, region + grid_step * push_box, corner_at)
    result = lax.fori_loop(0, SLOTS_ALL, deposit, stepped)
    return (result, settled, bending)
```

```python
import functools
import math

import jax
import jax.numpy as jnp
from jax import lax
from jax.experimental import pallas as pl
from jax.experimental.pallas import tpu as pltpu
from jax.sharding import PartitionSpec as P

ITERS = 12

box_step = 0.25
pseudo_step = 0.3
weno_floor = 1e-06
band_width = 1.5
tension = 2.0
grid_step = 0.2
viscosity = 0.1
normal_floor = 0.5
speck = 1.1e-19

SUB = 8
CHUNK = 8
DEPOSIT = 4
MIB = 1 << 20

MESH = pl.DeviceIdType.MESH
f32, bf16 = jnp.float32, jnp.bfloat16


def iota(shape, dim):
    return lax.broadcasted_iota(jnp.int32, shape, dim)


def halves(x):
    high = x.astype(bf16)
    return jnp.concatenate([high, (x - high.astype(f32)).astype(bf16)], axis=1)


def ones(mask):
    return jnp.where(mask, 1.0, 0.0).astype(bf16)


class Box:
    def __init__(self, edge, lanes, slots):
        self.edge, self.lanes = edge, lanes
        self.per = lanes // edge
        self.groups = slots // self.per
        self.halves = edge // SUB
        self.here = pl.ds(SUB, edge)
        self.below = pl.ds(SUB - 1, edge)
        self.above = pl.ds(SUB + 1, edge)
        self.block8 = iota((SUB, lanes), 1) // edge
        self.row8 = iota((SUB, lanes), 0)
        self.block = iota((edge, lanes), 1) // edge
        k_at = iota((edge, lanes), 1) % edge
        self.k_first, self.k_last = k_at == 0, k_at == edge - 1
        self.k_at = k_at

    def prev(self, x, n=1):
        return pltpu.roll(x, n, 1)

    def next(self, x, n=1):
        return pltpu.roll(x, self.lanes - n, 1)

    def swap_blocks(self, x):
        x = pltpu.roll(x, 0, 1, stride=self.edge, stride_axis=0)
        for b in (1, 2, 4):
            x = jnp.where((self.block8 & b) != 0, pltpu.roll(x, SUB - b, 0), x)
        x = pltpu.roll(x, 0, 1, stride=self.edge, stride_axis=0)
        x = pltpu.roll(x, 4, 0)
        for b in (1, 2):
            x = jnp.where((self.row8 & b) != 0, pltpu.roll(x, b, 0), pltpu.roll(x, SUB - b, 0))
        return pltpu.roll(x, 1, 0)

    def put(self, ref, i, g, value):
        last = SUB + self.edge
        ref[i, g, self.here] = value
        ref[i, g, SUB - 1 : SUB] = value[:1]
        ref[i, g, last : last + 1] = value[self.edge - 1 :]


def fetch_levels(box, native, lev):
    edge, per = box.edge, box.per

    def fetch(i, carry):
        for g in range(box.groups):
            pieces = [
                box.swap_blocks(native[h, pl.ds(g * per * edge + i, per, stride=edge), :])
                for h in range(box.halves)
            ]
            box.put(lev, i, g, 2.0 * jnp.concatenate(pieces, axis=0))
        return carry

    lax.fori_loop(0, edge, fetch, 0, unroll=4)


def window_matrix(box, corners):
    lanes, edge = box.lanes, box.edge
    columns = []
    for g in range(box.groups):
        block = iota((1, lanes), 1) // edge
        first = jnp.zeros((1, lanes), jnp.int32)
        for s in range(box.per):
            first = jnp.where(block == s, corners[2, g * box.per + s], first)
        wanted = first + iota((1, lanes), 1) % edge
        columns.append(ones(iota((lanes, lanes), 0) == wanted))
    both = jnp.concatenate(columns, axis=1)
    return jnp.concatenate([both, both], axis=0)


def shift_matrix(lanes):
    z, l = iota((lanes, lanes), 0), iota((lanes, lanes), 1)
    both = jnp.concatenate([ones(z == l - 1), ones(z == l + 1)], axis=1)
    return jnp.concatenate([both, both], axis=0)


def gather_motion(box, corners, wide, mot):
    edge, per = box.edge, box.per
    for g in range(box.groups):
        places = [[corners[d, g * per + s] for d in range(2)] for s in range(per)]

        def gather(i, carry, g=g, places=places):
            for c in range(3):
                acc = None
                for s in range(per):
                    rows = wide[c, g, places[s][0] + i, pl.ds(places[s][1], edge), :]
                    acc = rows if acc is None else jnp.where(box.block == s, rows, acc)
                mot[c, i, g] = acc
            return carry

        lax.fori_loop(0, edge, gather, 0, unroll=2)


def lean(e1, e2, e3, e4):
    floor = 3.0 * weno_floor
    s2, s3 = e2 * e2, e3 * e3
    b1 = e1 * (e1 - 2.75 * e2) + (2.5 * s2 + floor)
    b2 = e2 * (e2 - 1.25 * e3) + (s3 + floor)
    b3 = e4 * (e4 - 2.75 * e3) + (2.5 * s3 + floor)
    a1, a2, a3 = 3.0 * (b1 * b1), b2 * b2, b3 * b3
    t = 2.0 * e3
    p = a2 * a3
    top = p * (e1 - 2.5 * e2) + a1 * (a2 * (0.5 * e4 - t) - a3 * (e2 + t))
    return top, p + a1 * (a2 + 2.0 * a3)


def advect_levels(box, lev, mi, di, mj, dj, mot, psa, sign, rate):
    edge, here, below, above = box.edge, box.here, box.below, box.above
    zero = jnp.zeros((edge, box.lanes), f32)
    last = SUB + edge

    for g in range(box.groups):
        mi[0, g] = zero
        for n in (0, 1, edge + 1, edge + 2, edge + 3):
            di[n, g] = zero

    def rise(i, carry):
        for g in range(box.groups):
            @pl.when(i > 0)
            def _(g=g):
                mi[i, g] = lev[i, g, here] - lev[i - 1, g, here]

            step = lev[i, g, here] - lev[i, g, below]
            mj[i, g, here] = step
            mj[i, g, last : last + 1] = step[edge - 1 :]
        return carry

    lax.fori_loop(0, edge, rise, 0, unroll=True)
    for g in range(box.groups):
        mi[edge, g] = mi[edge - 1, g]

    def bow(i, carry):
        for g in range(box.groups):
            if_last = mi[i, g] - mi[i + 1, g]
            di[i + 2, g] = if_last
            dj[i, g, pl.ds(0, SUB)] = zero[:SUB]
            dj[i, g, pl.ds(last, SUB)] = zero[:SUB]
            dj[i, g, here] = mj[i, g, here] - mj[i, g, above]
        return carry

    lax.fori_loop(0, edge, bow, 0, unroll=4)

    k_low2 = box.k_at >= 2
    k_up1 = box.k_at < edge - 1
    k_up2 = box.k_at < edge - 2

    def advect(i, carry):
        for g in range(box.groups):
            level = lev[i, g, here]
            drift = turn = None
            for d in range(3):
                if d == 0:
                    m0, m1 = mi[i, g], mi[i + 1, g]
                    ds = [di[i + n, g] for n in range(5)]
                elif d == 1:
                    m0, m1 = mj[i, g, here], mj[i, g, above]
                    ds = [dj[i, g, pl.ds(SUB - 2 + n, edge)] for n in range(5)]
                else:
                    m0 = jnp.where(box.k_first, 0.0, level - box.prev(level))
                    m1 = jnp.where(box.k_last, m0, box.next(m0))
                    mid = m0 - m1
                    ds = [
                        jnp.where(k_low2, box.prev(mid, 2), 0.0),
                        box.prev(mid, 1),
                        mid,
                        jnp.where(k_up1, box.next(mid, 1), 0.0),
                        jnp.where(k_up2, box.next(mid, 2), 0.0),
                    ]
                speed = mot[d, i, g]
                pos = speed > 0.0
                e1 = jnp.where(pos, ds[0], ds[4])
                e2 = jnp.where(pos, ds[1], ds[3])
                e4 = jnp.where(pos, ds[3], ds[1])
                top, bottom = lean(e1, e2, ds[2], e4)
                part = speed * jnp.where(pos, m0, m1)
                extra = jnp.abs(speed) * (top / bottom)
                drift = part if drift is None else drift + part
                turn = extra if turn is None else turn + extra
            out = 0.5 * level - (0.5 * box_step) * drift - (box_step / 6.0) * turn
            box.put(psa, i, g, out)
            sign[i, g] = jnp.where(out > 0.0, 1.0, -1.0)
            rate[i, g] = pseudo_step * out * lax.rsqrt(out * out + 1.0)
        return carry

    lax.fori_loop(0, edge, advect, 0, unroll=2)


def reinitialize(box, psa, psb, sign, rate):
    edge, here, below, above = box.edge, box.here, box.below, box.above
    low = jnp.where(box.k_first, 0.0, 1.0)
    high = jnp.where(box.k_last, 0.0, 1.0)

    def sweep(src, dst):
        for i in range(edge):
            for g in range(box.groups):
                cur = src[i, g, here]
                s, r = sign[i, g], rate[i, g]
                signed = s * cur
                x = signed - jnp.minimum(
                    s * src[max(i - 1, 0), g, here], s * src[min(i + 1, edge - 1), g, here]
                )
                y = signed - jnp.minimum(s * src[i, g, below], s * src[i, g, above])
                z = jnp.maximum(
                    (s * low) * (cur - box.prev(cur)), (s * high) * (cur - box.next(cur))
                )
                x = jnp.maximum(x, speck)
                y, z = jnp.maximum(y, 0.0), jnp.maximum(z, 0.0)
                total = x * x + y * y + z * z
                box.put(dst, i, g, (cur + r) - r * (total * lax.rsqrt(total)))

    def two_sweeps(n, carry):
        sweep(psa, psb)
        sweep(psb, psa)
        return carry

    lax.fori_loop(0, ITERS // 2, two_sweeps, 0)


def curve_levels(box, owners, psi, nx, ny, part, force, native_a, native_b):
    edge, per, here, below, above = box.edge, box.per, box.here, box.below, box.above

    def spread(x):
        return jnp.where(box.k_last, x, box.next(x)) - jnp.where(box.k_first, x, box.prev(x))

    def bend(i, carry):
        for g in range(box.groups):
            cur = psi[i, g, here]
            c0 = psi[jnp.minimum(i + 1, edge - 1), g, here] - psi[jnp.maximum(i - 1, 0), g, here]
            c1 = psi[i, g, above] - psi[i, g, below]
            c2 = spread(cur)
            floor = 4.0 * normal_floor * normal_floor
            inverse = lax.rsqrt(jnp.maximum(c0 * c0 + c1 * c1 + c2 * c2, floor))
            nx[i, g] = c0 * inverse
            box.put(ny, i, g, c1 * inverse)
            part[i, g] = spread(c2 * inverse)
            for d, c in enumerate((c0, c1, c2)):
                force[d, i, g] = c
        return carry

    lax.fori_loop(0, edge, bend, 0, unroll=2)

    alive = []
    for g in range(box.groups):
        live = jnp.zeros((edge, box.lanes), f32)
        for s in range(per):
            on = jnp.where(owners[g * per + s] >= 0, 1.0, 0.0)
            live = jnp.where(box.block == s, on, live)
        alive.append(live)

    def push(i, carry):
        for g in range(box.groups):
            live = alive[g]
            level = psi[i, g, here] * live
            ends = nx[jnp.minimum(i + 1, edge - 1), g] - nx[jnp.maximum(i - 1, 0), g]
            curve = (0.5 * live) * (ends + (ny[i, g, above] - ny[i, g, below]) + part[i, g])
            for h in range(box.halves):
                at = pl.ds(g * per * edge + i, per, stride=edge)
                rows = slice(h * SUB, (h + 1) * SUB)
                native_a[h, at, :] = box.swap_blocks(level[rows])
                native_b[h, at, :] = box.swap_blocks(curve[rows])
            ratio = level * (1.0 / band_width)
            scale = 0.5 * grid_step * tension / (band_width * math.sqrt(math.pi))
            strength = scale * curve * jnp.exp(-(ratio * ratio)) * live
            for d in range(3):
                force[d, i, g] = force[d, i, g] * strength
        return carry

    lax.fori_loop(0, edge, push, 0, unroll=2)


class Grid:
    def __init__(self, xs, ys, lanes):
        self.xs, self.ys, self.lanes = xs, ys, lanes
        self.here = pl.ds(SUB, ys)
        self.below = pl.ds(SUB - 1, ys)
        self.above = pl.ds(SUB + 1, ys)
        self.rows = ys + 2 * SUB
        self.shape = (3, xs + 2, self.rows, lanes)
        self.lane = iota((ys, lanes), 1)
        self.group = self.lane // 4

    def row_of(self, ref, c, x, row):
        flat = ref.reshape(3 * (self.xs + 2) * self.rows, self.lanes)
        return flat.at[pl.ds((c * (self.xs + 2) + x) * self.rows + row, SUB, stride=self.rows), :]

    def fill_rows(self, ref, low, high):
        for c in range(3):
            for x in range(0, self.xs, SUB):
                part = pl.ds(x, SUB)
                self.row_of(ref, c, x + 1, SUB - 1)[...] = low[c, part]
                self.row_of(ref, c, x + 1, SUB + self.ys)[...] = high[c, part]

    def take_rows(self, ref, ysend):
        for c in range(3):
            for x in range(0, self.xs, SUB):
                part = pl.ds(x, SUB)
                ysend[0, c, part] = self.row_of(ref, c, x + 1, SUB + self.ys - 1)[...]
                ysend[1, c, part] = self.row_of(ref, c, x + 1, SUB)[...]

    def combine(self, zlow, zhigh, comb):
        for c in range(3):
            comb[c] = jnp.where(
                self.lane % 4 == 0,
                pltpu.roll(zhigh[c], self.lanes - 1, 1),
                pltpu.roll(zlow[c], 1, 1),
            )

    def packed(self, value, x, acc):
        return jnp.where(self.group == x, pltpu.roll(value, 4 * x + 1, 1), acc)

    def shift(self, src, shifts, near, slot, first):
        left = jnp.concatenate(
            [halves(src[c, 1 + first + n, self.here]) for c in range(3) for n in range(CHUNK)], axis=0
        )
        both = jnp.dot(left, shifts[...], preferred_element_type=f32)
        for c in range(3):
            for n in range(CHUNK):
                at = (c * CHUNK + n) * self.ys
                for e in range(2):
                    near[slot, c, n, e] = both[at : at + self.ys, e * self.lanes : (e + 1) * self.lanes]

    def section(self, src, comb, shifts, near, scale, emit):
        h = scale * grid_step * viscosity
        chunks = self.xs // CHUNK

        def chunk(t, carry):
            slot = t % 2
            self.shift(src, shifts, near, 1 - slot, CHUNK * jnp.minimum(t + 1, chunks - 1))
            for n in range(CHUNK):
                x = CHUNK * t + n
                centre = [src[c, x + 1, self.here] for c in range(3)]
                w = [(0.5 * scale * grid_step) * v for v in centre]
                up, down = [h - v for v in w], [h + v for v in w]
                rim = jnp.where(self.lane == 0, down[2], jnp.where(self.lane == self.lanes - 1, up[2], 0.0))
                for c in range(3):
                    halo = pltpu.roll(comb[c], self.lanes - 1 - 4 * x, 1)
                    value = (
                        (scale - 6.0 * h) * centre[c]
                        + up[0] * src[c, x + 2, self.here]
                        + down[0] * src[c, x, self.here]
                        + up[1] * src[c, x + 1, self.above]
                        + down[1] * src[c, x + 1, self.below]
                        + up[2] * near[slot, c, n, 1]
                        + down[2] * near[slot, c, n, 0]
                        + rim * halo
                    )
                    emit(c, x, value)
            return carry

        lax.fori_loop(0, chunks, chunk, 0)


def step_kernel(
    sizes, corners, owners, v_hbm, lev_hbm,
    vel, pred, yrecv1, zrecv1, force, native_a, native_b,
    yrecv0, zrecv0, ysend, zsend, comb, near, shifts, windows, wide,
    native, lev, mi, di, mj, dj, mot, psa, psb, sign, rate,
    local_sem, lev_sem, send_sem, recv_sem,
):
    _, xs, ys, lanes = v_hbm.shape
    grid = Grid(xs, ys, lanes)
    slots = corners.shape[1]
    edge = lev.shape[0]
    box = Box(edge, lanes, slots)
    inner = pl.ds(1, xs)
    levels = [
        pltpu.make_async_copy(lev_hbm.at[:, pl.ds(h * lanes, lanes)], native.at[h], lev_sem.at[h])
        for h in range(box.halves)
    ]
    for part in levels:
        part.start()
    load = pltpu.make_async_copy(v_hbm, vel.at[:, inner, grid.here], local_sem)
    load.start()
    ups, downs = [], []
    for axis in ("gx", "gy", "gz"):
        me, n = lax.axis_index(axis), sizes[axis]
        ups.append({axis: lax.rem(me + 1, n)})
        downs.append({axis: lax.rem(me + n - 1, n)})
    barrier = pltpu.get_barrier_semaphore()
    for target in ups + downs:
        pl.semaphore_signal(barrier, inc=1, device_id=target, device_id_type=MESH)
    shifts[...] = shift_matrix(lanes)
    windows[...] = window_matrix(box, corners)
    for part in levels:
        part.wait()
    fetch_levels(box, native, lev)
    load.wait()

    def exchange(r, src, yrecv, zrecv):
        copies = []

        def send(n, src, dst, target):
            copy = pltpu.make_async_remote_copy(
                src_ref=src,
                dst_ref=dst,
                send_sem=send_sem.at[r, n],
                recv_sem=recv_sem.at[r, n],
                device_id=target,
                device_id_type=MESH,
            )
            copy.start()
            copies.append(copy)

        send(0, src.at[:, xs, grid.here], src.at[:, 0, grid.here], ups[0])
        send(1, src.at[:, 1, grid.here], src.at[:, xs + 1, grid.here], downs[0])
        send(2, ysend.at[r, 0], yrecv.at[0], ups[1])
        send(3, ysend.at[r, 1], yrecv.at[1], downs[1])
        send(4, zsend.at[r], zrecv.at[0], ups[2])
        send(5, zsend.at[r], zrecv.at[1], downs[2])
        return copies

    for c in range(3):
        zsend[0, c] = jnp.zeros((ys, lanes), f32)
        zsend[1, c] = jnp.zeros((ys, lanes), f32)
    span = xs // 2

    def spread(t, carry):
        left = []
        for c in range(3):
            acc = zsend[0, c]
            for n in range(span):
                x = span * t + n
                value = vel[c, x + 1, grid.here]
                left.append(halves(value))
                acc = grid.packed(value, x, acc)
            zsend[0, c] = acc
        both = jnp.dot(jnp.concatenate(left, axis=0), windows[...], preferred_element_type=f32)
        for c in range(3):
            for n in range(span):
                at = (c * span + n) * ys
                for g in range(box.groups):
                    wide[c, g, span * t + n] = both[at : at + ys, g * lanes : (g + 1) * lanes]
        return carry

    lax.fori_loop(0, xs // span, spread, 0)
    grid.take_rows(vel, ysend.at[0])
    pl.semaphore_wait(barrier, 6)
    copies = exchange(0, vel, yrecv0, zrecv0)
    gather_motion(box, corners, wide, mot)
    advect_levels(box, lev, mi, di, mj, dj, mot, psa, sign, rate)
    grid.shift(vel, shifts, near, 0, 0)
    for copy in copies:
        copy.wait()
    grid.fill_rows(vel, yrecv0.at[0], yrecv0.at[1])
    grid.combine(zrecv0.at[0], zrecv0.at[1], comb)

    def first(c, x, value):
        pred[c, x + 1, grid.here] = value
        zsend[1, c] = grid.packed(value, x, zsend[1, c])

    grid.section(vel, comb, shifts, near, 1.0, first)
    grid.take_rows(pred, ysend.at[1])
    copies = exchange(1, pred, yrecv1, zrecv1)
    reinitialize(box, psa, psb, sign, rate)
    curve_levels(box, owners, psa, mi, mj, di, force, native_a, native_b)
    for copy in copies:
        copy.wait()


def kept(x):
    return pltpu.with_memory_space_constraint(x, pltpu.HBM)


def step_call(velocity, box_level, corners, owner_list):
    sizes = {axis: lax.axis_size(axis) for axis in ("gx", "gy", "gz")}
    _, xs, ys, lanes = velocity.shape
    slots, edge, plane = box_level.shape
    groups = slots * edge // lanes
    vmem = pltpu.VMEM
    grid_shape = (3, xs + 2, ys + 2 * SUB, lanes)
    tall = (edge, groups, edge + 2 * SUB, lanes)
    flat = (edge, groups, edge, lanes)
    native = (plane // lanes, slots * edge, lanes)
    smem = pl.BlockSpec(memory_space=pltpu.SMEM)
    return pl.pallas_call(
        functools.partial(step_kernel, sizes),
        out_shape=(
            vmem(grid_shape, f32),
            vmem(grid_shape, f32),
            vmem((2, 3, xs, lanes), f32),
            vmem((2, 3, ys, lanes), f32),
            vmem((3,) + flat, f32),
            vmem(native, f32),
            vmem(native, f32),
        ),
        in_specs=[smem, smem, pl.BlockSpec(memory_space=pltpu.HBM), pl.BlockSpec(memory_space=pltpu.HBM)],
        out_specs=(pl.BlockSpec(memory_space=vmem),) * 7,
        scratch_shapes=[
            vmem((2, 3, xs, lanes), f32),
            vmem((2, 3, ys, lanes), f32),
            vmem((2, 2, 3, xs, lanes), f32),
            vmem((2, 3, ys, lanes), f32),
            vmem((3, ys, lanes), f32),
            vmem((2, 3, CHUNK, 2, ys, lanes), f32),
            vmem((2 * lanes, 2 * lanes), bf16),
            vmem((2 * lanes, groups * lanes), bf16),
            vmem((3, groups, xs, ys, lanes), f32),
            vmem(native, f32),
            vmem(tall, f32),
            vmem((edge + 1,) + flat[1:], f32),
            vmem((edge + 4,) + flat[1:], f32),
            vmem(tall, f32),
            vmem(tall, f32),
            vmem((3,) + flat, f32),
            vmem(tall, f32),
            vmem(tall, f32),
            vmem(flat, f32),
            vmem(flat, f32),
            pltpu.SemaphoreType.DMA(()),
            pltpu.SemaphoreType.DMA((plane // lanes,)),
            pltpu.SemaphoreType.DMA((2, 6)),
            pltpu.SemaphoreType.DMA((2, 6)),
        ],
        compiler_params=pltpu.CompilerParams(
            collective_id=0, has_side_effects=True, vmem_limit_bytes=36 * MIB
        ),
    )(corners, owner_list, kept(velocity), kept(box_level.reshape(slots * edge, plane)))


def force_kernel(
    corners, vel, pred, yrecv, zrecv, force, native_a, native_b,
    o_hbm, set_hbm, ben_hbm,
    src, o_ref, comb, near, shifts, out_sem, small_sem,
):
    _, xs, ys, lanes = o_ref.shape
    grid = Grid(xs, ys, lanes)
    slots = corners.shape[1]
    edge = force.shape[1]
    box = Box(edge, lanes, slots)
    per = box.per
    stores = []
    for h in range(box.halves):
        part_h = pl.ds(h * lanes, lanes)
        stores.append(pltpu.make_async_copy(native_a.at[h], set_hbm.at[:, part_h], small_sem.at[0, h]))
        stores.append(pltpu.make_async_copy(native_b.at[h], ben_hbm.at[:, part_h], small_sem.at[1, h]))
    for copy in stores:
        copy.start()
    shifts[...] = shift_matrix(lanes)
    grid.combine(zrecv.at[0], zrecv.at[1], comb)
    grid.shift(pred, shifts, near, 0, 0)

    def second(c, x, value):
        o_ref[c, x] = 0.5 * vel[c, x + 1, grid.here] + value

    grid.fill_rows(pred, yrecv.at[0], yrecv.at[1])
    grid.section(pred, comb, shifts, near, 0.5, second)

    wide = iota((edge, lanes), 1)

    def deposit_slot(n, carry):
        g, s = n // per, n % per
        ax, ay, az = corners[0, n], corners[1, n], corners[2, n]
        turn = lax.rem(az + lanes - s * edge, lanes)
        inside = jnp.logical_and(wide >= az, wide < az + edge)

        for i in range(0, edge, DEPOSIT):
            spots = [(c, i + t) for t in range(DEPOSIT) for c in range(3)]
            blocks = [pltpu.roll(force[c, q, g], turn, 1) for c, q in spots]
            olds = [o_ref[c, ax + q, pl.ds(ay, edge), :] for c, q in spots]
            news = [old + jnp.where(inside, block, 0.0) for old, block in zip(olds, blocks)]
            for (c, q), new in zip(spots, news):
                o_ref[c, ax + q, pl.ds(ay, edge), :] = new
        return carry

    lax.fori_loop(0, slots, deposit_slot, 0)
    for c in range(3):
        stores.append(pltpu.make_async_copy(o_ref.at[c], o_hbm.at[c], out_sem.at[c]))
        stores[-1].start()
    for copy in stores:
        copy.wait()


def force_call(shapes, block, corners, handed):
    slots, edge, plane = shapes
    _, xs, ys, lanes = block
    flat = (slots * edge, plane)
    whole = pl.BlockSpec(memory_space=pltpu.VMEM)
    smem = pl.BlockSpec(memory_space=pltpu.SMEM)
    handed = [pltpu.with_memory_space_constraint(a, pltpu.VMEM) for a in handed]
    result, settled, bending = pl.pallas_call(
        force_kernel,
        out_shape=(
            jax.ShapeDtypeStruct(block, f32),
            jax.ShapeDtypeStruct(flat, f32),
            jax.ShapeDtypeStruct(flat, f32),
        ),
        in_specs=[smem] + [whole] * 7,
        out_specs=(pl.BlockSpec(memory_space=pltpu.HBM),) * 3,
        scratch_shapes=[
            pltpu.VMEM((SUB, lanes), f32),
            pltpu.VMEM(block, f32),
            pltpu.VMEM((3, ys, lanes), f32),
            pltpu.VMEM((2, 3, CHUNK, 2, ys, lanes), f32),
            pltpu.VMEM((2 * lanes, 2 * lanes), bf16),
            pltpu.SemaphoreType.DMA((3,)),
            pltpu.SemaphoreType.DMA((2, plane // lanes)),
        ],
        compiler_params=pltpu.CompilerParams(vmem_limit_bytes=24 * MIB),
    )(corners, *handed)
    return result, settled.reshape(shapes), bending.reshape(shapes)


def local(velocity, box_level, corners, owner_list):
    turned, owner_list = kept(corners.T), kept(owner_list)
    handed = step_call(velocity, box_level, turned, owner_list)
    return force_call(box_level.shape, velocity.shape, turned, handed)


def solution(mesh):
    placed = (
        P(None, "gx", "gy", "gz"),
        P(("gx", "gy", "gz"), None, None),
        P(("gx", "gy", "gz"), None),
        P(("gx", "gy", "gz")),
    )
    return jax.shard_map(
        local,
        mesh=mesh,
        in_specs=placed,
        out_specs=(
            P(None, "gx", "gy", "gz"),
            P(("gx", "gy", "gz"), None, None),
            P(("gx", "gy", "gz"), None, None),
        ),
        check_vma=False,
    )
```

```python
import functools
import math

import jax
import jax.numpy as jnp
from jax import lax
from jax.experimental import pallas as pl
from jax.experimental.pallas import tpu as pltpu
from jax.sharding import PartitionSpec as P

ITERS = 12

box_step = 0.25
pseudo_step = 0.3
weno_floor = 1e-06
band_width = 1.5
tension = 2.0
grid_step = 0.2
viscosity = 0.1
normal_floor = 0.5
speck = 1.1e-19

SUB = 8
PLANES = 4
EARLY = 1
DEPOSIT = 4
TURN = 12
MIB = 1 << 20

MESH = pl.DeviceIdType.MESH
f32, bf16 = jnp.float32, jnp.bfloat16


def iota(shape, dim):
    return lax.broadcasted_iota(jnp.int32, shape, dim)


def halves(x):
    high = x.astype(bf16)
    return jnp.concatenate([high, (x - high.astype(f32)).astype(bf16)], axis=1)


def ones(mask):
    return jnp.where(mask, 1.0, 0.0).astype(bf16)


class Box:
    def __init__(self, edge, lanes, slots):
        self.edge, self.lanes = edge, lanes
        self.per = lanes // edge
        self.groups = slots // self.per
        self.halves = edge // SUB
        self.here = pl.ds(SUB, edge)
        self.below = pl.ds(SUB - 1, edge)
        self.above = pl.ds(SUB + 1, edge)
        self.block8 = iota((SUB, lanes), 1) // edge
        self.row8 = iota((SUB, lanes), 0)
        self.block = iota((edge, lanes), 1) // edge
        k_at = iota((edge, lanes), 1) % edge
        self.k_first, self.k_last = k_at == 0, k_at == edge - 1
        self.k_at = k_at

    def prev(self, x, n=1):
        return pltpu.roll(x, n, 1)

    def next(self, x, n=1):
        return pltpu.roll(x, self.lanes - n, 1)

    def swap_blocks(self, x):
        x = pltpu.roll(x, 0, 1, stride=self.edge, stride_axis=0)
        for b in (1, 2, 4):
            x = jnp.where((self.block8 & b) != 0, pltpu.roll(x, SUB - b, 0), x)
        x = pltpu.roll(x, 0, 1, stride=self.edge, stride_axis=0)
        x = pltpu.roll(x, 4, 0)
        for b in (1, 2):
            x = jnp.where((self.row8 & b) != 0, pltpu.roll(x, b, 0), pltpu.roll(x, SUB - b, 0))
        return pltpu.roll(x, 1, 0)

    def put(self, ref, i, g, value):
        last = SUB + self.edge
        ref[i, g, self.here] = value
        ref[i, g, SUB - 1 : SUB] = value[:1]
        ref[i, g, last : last + 1] = value[self.edge - 1 :]


def fetch_levels(box, native, lev):
    edge, per = box.edge, box.per

    def fetch(i, carry):
        for g in range(box.groups):
            pieces = [
                box.swap_blocks(native[h, pl.ds(g * per * edge + i, per, stride=edge), :])
                for h in range(box.halves)
            ]
            box.put(lev, i, g, 2.0 * jnp.concatenate(pieces, axis=0))
        return carry

    lax.fori_loop(0, edge, fetch, 0, unroll=True)


def window_matrix(box, corners):
    lanes, edge = box.lanes, box.edge
    columns = []
    for g in range(box.groups):
        block = iota((1, lanes), 1) // edge
        first = jnp.zeros((1, lanes), jnp.int32)
        for s in range(box.per):
            first = jnp.where(block == s, corners[2, g * box.per + s], first)
        wanted = first + iota((1, lanes), 1) % edge
        columns.append(ones(iota((lanes, lanes), 0) == wanted))
    both = jnp.concatenate(columns, axis=1)
    return jnp.concatenate([both, both], axis=0)


def shift_matrix(lanes):
    z, l = iota((lanes, lanes), 0), iota((lanes, lanes), 1)
    both = jnp.concatenate([ones(z == l - 1), ones(z == l + 1)], axis=1)
    return jnp.concatenate([both, both], axis=0)


def gather_motion(box, corners, wide, mot):
    edge, per = box.edge, box.per
    for g in range(box.groups):
        places = [[corners[d, g * per + s] for d in range(2)] for s in range(per)]

        def gather(i, carry, g=g, places=places):
            for c in range(3):
                acc = None
                for s in range(per):
                    rows = wide[c, g, places[s][0] + i, pl.ds(places[s][1], edge), :]
                    acc = rows if acc is None else jnp.where(box.block == s, rows, acc)
                mot[c, i, g] = acc
            return carry

        lax.fori_loop(0, edge, gather, 0, unroll=4)


def lean(e1, e2, e3, e4):
    floor = 3.0 * weno_floor
    s2, s3 = e2 * e2, e3 * e3
    b1 = e1 * (e1 - 2.75 * e2) + (2.5 * s2 + floor)
    b2 = e2 * (e2 - 1.25 * e3) + (s3 + floor)
    b3 = e4 * (e4 - 2.75 * e3) + (2.5 * s3 + floor)
    a1, a2, a3 = 3.0 * (b1 * b1), b2 * b2, b3 * b3
    t = 2.0 * e3
    p = a2 * a3
    top = p * (e1 - 2.5 * e2) + a1 * (a2 * (0.5 * e4 - t) - a3 * (e2 + t))
    return top, p + a1 * (a2 + 2.0 * a3)


def advect_levels(box, lev, mi, di, mj, dj, mot, psa, sign, rate):
    edge, here, below, above = box.edge, box.here, box.below, box.above
    zero = jnp.zeros((edge, box.lanes), f32)
    last = SUB + edge

    for g in range(box.groups):
        mi[0, g] = zero
        for n in (0, 1, edge + 1, edge + 2, edge + 3):
            di[n, g] = zero

    def rise(i, carry):
        for g in range(box.groups):
            @pl.when(i > 0)
            def _(g=g):
                mi[i, g] = lev[i, g, here] - lev[i - 1, g, here]

            step = lev[i, g, here] - lev[i, g, below]
            mj[i, g, here] = step
            mj[i, g, last : last + 1] = step[edge - 1 :]
        return carry

    lax.fori_loop(0, edge, rise, 0, unroll=True)
    for g in range(box.groups):
        mi[edge, g] = mi[edge - 1, g]

    def bow(i, carry):
        for g in range(box.groups):
            if_last = mi[i, g] - mi[i + 1, g]
            di[i + 2, g] = if_last
            dj[i, g, pl.ds(0, SUB)] = zero[:SUB]
            dj[i, g, pl.ds(last, SUB)] = zero[:SUB]
            dj[i, g, here] = mj[i, g, here] - mj[i, g, above]
        return carry

    lax.fori_loop(0, edge, bow, 0, unroll=4)

    k_low2 = box.k_at >= 2
    k_up1 = box.k_at < edge - 1
    k_up2 = box.k_at < edge - 2

    def advect(i, carry):
        for g in range(box.groups):
            level = lev[i, g, here]
            drift = turn = None
            for d in range(3):
                if d == 0:
                    m0, m1 = mi[i, g], mi[i + 1, g]
                    ds = [di[i + n, g] for n in range(5)]
                elif d == 1:
                    m0, m1 = mj[i, g, here], mj[i, g, above]
                    ds = [dj[i, g, pl.ds(SUB - 2 + n, edge)] for n in range(5)]
                else:
                    m0 = jnp.where(box.k_first, 0.0, level - box.prev(level))
                    m1 = jnp.where(box.k_last, m0, box.next(m0))
                    mid = m0 - m1
                    ds = [
                        jnp.where(k_low2, box.prev(mid, 2), 0.0),
                        box.prev(mid, 1),
                        mid,
                        jnp.where(k_up1, box.next(mid, 1), 0.0),
                        jnp.where(k_up2, box.next(mid, 2), 0.0),
                    ]
                speed = mot[d, i, g]
                pos = speed > 0.0
                e1 = jnp.where(pos, ds[0], ds[4])
                e2 = jnp.where(pos, ds[1], ds[3])
                e4 = jnp.where(pos, ds[3], ds[1])
                top, bottom = lean(e1, e2, ds[2], e4)
                part = speed * jnp.where(pos, m0, m1)
                extra = jnp.abs(speed) * (top / bottom)
                drift = part if drift is None else drift + part
                turn = extra if turn is None else turn + extra
            out = 0.5 * level - (0.5 * box_step) * drift - (box_step / 6.0) * turn
            box.put(psa, i, g, out)
            sign[i, g] = jnp.where(out > 0.0, 1.0, -1.0)
            rate[i, g] = pseudo_step * out * lax.rsqrt(out * out + 1.0)
        return carry

    lax.fori_loop(0, edge, advect, 0, unroll=8)


def reinitialize(box, pairs, psa, psb, sign, rate):
    edge, here, below, above = box.edge, box.here, box.below, box.above
    low = jnp.where(box.k_first, 0.0, 1.0)
    high = jnp.where(box.k_last, 0.0, 1.0)

    def sweep(src, dst):
        for i in range(edge):
            for g in range(box.groups):
                cur = src[i, g, here]
                s, r = sign[i, g], rate[i, g]
                signed = s * cur
                x = signed - jnp.minimum(
                    s * src[max(i - 1, 0), g, here], s * src[min(i + 1, edge - 1), g, here]
                )
                y = signed - jnp.minimum(s * src[i, g, below], s * src[i, g, above])
                z = jnp.maximum(
                    (s * low) * (cur - box.prev(cur)), (s * high) * (cur - box.next(cur))
                )
                x = jnp.maximum(x, speck)
                y, z = jnp.maximum(y, 0.0), jnp.maximum(z, 0.0)
                total = x * x + y * y + z * z
                box.put(dst, i, g, (cur + r) - r * (total * lax.rsqrt(total)))

    def two_sweeps(n, carry):
        sweep(psa, psb)
        sweep(psb, psa)
        return carry

    lax.fori_loop(0, pairs, two_sweeps, 0)


def curve_levels(box, owners, psi, nx, ny, part, force, native_a, native_b):
    edge, per, here, below, above = box.edge, box.per, box.here, box.below, box.above

    def spread(x):
        return jnp.where(box.k_last, x, box.next(x)) - jnp.where(box.k_first, x, box.prev(x))

    def bend(i, carry):
        for g in range(box.groups):
            cur = psi[i, g, here]
            c0 = psi[jnp.minimum(i + 1, edge - 1), g, here] - psi[jnp.maximum(i - 1, 0), g, here]
            c1 = psi[i, g, above] - psi[i, g, below]
            c2 = spread(cur)
            floor = 4.0 * normal_floor * normal_floor
            inverse = lax.rsqrt(jnp.maximum(c0 * c0 + c1 * c1 + c2 * c2, floor))
            nx[i, g] = c0 * inverse
            box.put(ny, i, g, c1 * inverse)
            part[i, g] = spread(c2 * inverse)
            for d, c in enumerate((c0, c1, c2)):
                force[d, i, g] = c
        return carry

    lax.fori_loop(0, edge, bend, 0, unroll=8)

    alive = []
    for g in range(box.groups):
        live = jnp.zeros((edge, box.lanes), f32)
        for s in range(per):
            on = jnp.where(owners[g * per + s] >= 0, 1.0, 0.0)
            live = jnp.where(box.block == s, on, live)
        alive.append(live)

    def push(i, carry):
        for g in range(box.groups):
            live = alive[g]
            level = psi[i, g, here] * live
            ends = nx[jnp.minimum(i + 1, edge - 1), g] - nx[jnp.maximum(i - 1, 0), g]
            curve = (0.5 * live) * (ends + (ny[i, g, above] - ny[i, g, below]) + part[i, g])
            for h in range(box.halves):
                at = pl.ds(g * per * edge + i, per, stride=edge)
                rows = slice(h * SUB, (h + 1) * SUB)
                native_a[h, at, :] = box.swap_blocks(level[rows])
                native_b[h, at, :] = box.swap_blocks(curve[rows])
            ratio = level * (1.0 / band_width)
            scale = 0.5 * grid_step * tension / (band_width * math.sqrt(math.pi))
            strength = scale * curve * jnp.exp(-(ratio * ratio)) * live
            for d in range(3):
                force[d, i, g] = force[d, i, g] * strength
        return carry

    lax.fori_loop(0, edge, push, 0, unroll=8)


class Grid:
    def __init__(self, xs, ys, lanes):
        self.xs, self.ys, self.lanes = xs, ys, lanes
        self.here = pl.ds(SUB, ys)
        self.below = pl.ds(SUB - 1, ys)
        self.above = pl.ds(SUB + 1, ys)
        self.rows = ys + 2 * SUB
        self.shape = (3, xs + 2, self.rows, lanes)
        self.lane = iota((ys, lanes), 1)
        self.group = self.lane // 4

    def row_of(self, ref, c, x, row):
        flat = ref.reshape(3 * (self.xs + 2) * self.rows, self.lanes)
        return flat.at[pl.ds((c * (self.xs + 2) + x) * self.rows + row, SUB, stride=self.rows), :]

    def fill_rows(self, ref, low, high):
        for c in range(3):
            for x in range(0, self.xs, SUB):
                part = pl.ds(x, SUB)
                self.row_of(ref, c, x + 1, SUB - 1)[...] = low[c, part]
                self.row_of(ref, c, x + 1, SUB + self.ys)[...] = high[c, part]

    def take_rows(self, ref, ysend):
        for c in range(3):
            for x in range(0, self.xs, SUB):
                part = pl.ds(x, SUB)
                ysend[0, c, part] = self.row_of(ref, c, x + 1, SUB + self.ys - 1)[...]
                ysend[1, c, part] = self.row_of(ref, c, x + 1, SUB)[...]

    def combine(self, zlow, zhigh, comb):
        for c in range(3):
            comb[c] = jnp.where(
                self.lane % 4 == 0,
                pltpu.roll(zhigh[c], self.lanes - 1, 1),
                pltpu.roll(zlow[c], 1, 1),
            )

    def pack(self, value, c, x, y, zsend):
        tile = pl.ds(y, SUB)
        turned = pltpu.roll(value, 4 * x + 1, 1)
        zsend[c, tile] = jnp.where(self.group[:SUB] == x, turned, zsend[c, tile])

    def shift(self, src, shifts, near):
        span = self.xs // 2

        def part(t, carry):
            left = [halves(src[c, 1 + span * t + n, self.here]) for c in range(3) for n in range(span)]
            both = jnp.dot(jnp.concatenate(left, axis=0), shifts[...], preferred_element_type=f32)
            for c in range(3):
                for n in range(span):
                    at = (c * span + n) * self.ys
                    for e in range(2):
                        near[c, span * t + n, e] = both[at : at + self.ys, e * self.lanes : (e + 1) * self.lanes]
            return carry

        lax.fori_loop(0, 2, part, 0)

    def section(self, src, comb, near, scale, emit):
        h = scale * grid_step * viscosity
        lane = self.lane[:SUB]
        first, last = lane == 0, lane == self.lanes - 1

        def plane(x, carry):
            for y in range(0, self.ys, SUB):
                rows, tile = pl.ds(SUB + y, SUB), pl.ds(y, SUB)
                centre = [src[c, x + 1, rows] for c in range(3)]
                w = [(0.5 * scale * grid_step) * v for v in centre]
                up, down = [h - v for v in w], [h + v for v in w]
                rim = jnp.where(first, down[2], jnp.where(last, up[2], 0.0))
                for c in range(3):
                    halo = pltpu.roll(comb[c, tile], self.lanes - 1 - 4 * x, 1)
                    value = (
                        (scale - 6.0 * h) * centre[c]
                        + up[0] * src[c, x + 2, rows]
                        + down[0] * src[c, x, rows]
                        + up[1] * src[c, x + 1, pl.ds(SUB + y + 1, SUB)]
                        + down[1] * src[c, x + 1, pl.ds(SUB + y - 1, SUB)]
                        + up[2] * near[c, x, 1, tile]
                        + down[2] * near[c, x, 0, tile]
                        + rim * halo
                    )
                    emit(c, x, y, value)
            return carry

        lax.fori_loop(0, self.xs, plane, 0, unroll=PLANES)


def step_kernel(
    sizes, corners, owners, v_hbm, lev_hbm,
    vel, pred, near1, yrecv1, zrecv1, force, native_a, native_b,
    yrecv0, zrecv0, ysend, zsend, comb, near0, shifts, windows, wide,
    native, lev, mi, di, mj, dj, mot, psa, psb, sign, rate,
    local_sem, lev_sem, send_sem, recv_sem,
):
    _, xs, ys, lanes = v_hbm.shape
    grid = Grid(xs, ys, lanes)
    slots = corners.shape[1]
    edge = lev.shape[0]
    box = Box(edge, lanes, slots)
    inner = pl.ds(1, xs)
    loads = [
        pltpu.make_async_copy(v_hbm.at[c], vel.at[c, inner, grid.here], local_sem.at[c]) for c in range(3)
    ]
    levels = [
        pltpu.make_async_copy(lev_hbm.at[:, pl.ds(h * lanes, lanes)], native.at[h], lev_sem.at[h])
        for h in range(box.halves)
    ]
    for part in loads + levels:
        part.start()
    ups, downs = [], []
    for axis in ("gx", "gy", "gz"):
        me, n = lax.axis_index(axis), sizes[axis]
        ups.append({axis: lax.rem(me + 1, n)})
        downs.append({axis: lax.rem(me + n - 1, n)})
    barrier = pltpu.get_barrier_semaphore()
    for target in ups + downs:
        pl.semaphore_signal(barrier, inc=1, device_id=target, device_id_type=MESH)
    shifts[...] = shift_matrix(lanes)
    windows[...] = window_matrix(box, corners)

    def exchange(r, src, yrecv, zrecv):
        copies = []

        def send(n, src, dst, target):
            copy = pltpu.make_async_remote_copy(
                src_ref=src,
                dst_ref=dst,
                send_sem=send_sem.at[r, n],
                recv_sem=recv_sem.at[r, n],
                device_id=target,
                device_id_type=MESH,
            )
            copy.start()
            copies.append(copy)

        send(0, src.at[:, xs, grid.here], src.at[:, 0, grid.here], ups[0])
        send(1, src.at[:, 1, grid.here], src.at[:, xs + 1, grid.here], downs[0])
        send(2, ysend.at[r, 0], yrecv.at[0], ups[1])
        send(3, ysend.at[r, 1], yrecv.at[1], downs[1])
        send(4, zsend.at[r], zrecv.at[0], ups[2])
        send(5, zsend.at[r], zrecv.at[1], downs[2])
        return copies

    group = grid.group
    for c in range(3):
        loads[c].wait()

        def pack(x, acc, c=c):
            return jnp.where(group == x, pltpu.roll(vel[c, x + 1, grid.here], 4 * x + 1, 1), acc)

        zsend[0, c] = lax.fori_loop(0, xs, pack, jnp.zeros((ys, lanes), f32), unroll=8)
        zsend[1, c] = jnp.zeros((ys, lanes), f32)
    grid.take_rows(vel, ysend.at[0])
    span = xs // 2

    def spread(t, carry):
        left = [halves(vel[c, span * t + n + 1, grid.here]) for c in range(3) for n in range(span)]
        both = jnp.dot(jnp.concatenate(left, axis=0), windows[...], preferred_element_type=f32)
        for c in range(3):
            for n in range(span):
                at = (c * span + n) * ys
                for g in range(box.groups):
                    wide[c, g, span * t + n] = both[at : at + ys, g * lanes : (g + 1) * lanes]
        return carry

    pl.semaphore_wait(barrier, 6)
    copies = exchange(0, vel, yrecv0, zrecv0)
    lax.fori_loop(0, xs // span, spread, 0)
    for part in levels:
        part.wait()
    fetch_levels(box, native, lev)
    gather_motion(box, corners, wide, mot)
    advect_levels(box, lev, mi, di, mj, dj, mot, psa, sign, rate)
    grid.shift(vel, shifts, near0)
    reinitialize(box, EARLY, psa, psb, sign, rate)
    for copy in copies:
        copy.wait()
    grid.fill_rows(vel, yrecv0.at[0], yrecv0.at[1])
    grid.combine(zrecv0.at[0], zrecv0.at[1], comb)

    def first(c, x, y, value):
        pred[c, x + 1, pl.ds(SUB + y, SUB)] = value
        grid.pack(value, c, x, y, zsend.at[1])

    grid.section(vel, comb, near0, 1.0, first)
    grid.take_rows(pred, ysend.at[1])
    copies = exchange(1, pred, yrecv1, zrecv1)
    grid.shift(pred, shifts, near1)
    reinitialize(box, ITERS // 2 - EARLY, psa, psb, sign, rate)
    curve_levels(box, owners, psa, mi, mj, di, force, native_a, native_b)
    for copy in copies:
        copy.wait()


def kept(x):
    return pltpu.with_memory_space_constraint(x, pltpu.HBM)


def step_call(velocity, box_level, corners, owner_list):
    sizes = {axis: lax.axis_size(axis) for axis in ("gx", "gy", "gz")}
    _, xs, ys, lanes = velocity.shape
    slots, edge, plane = box_level.shape
    groups = slots * edge // lanes
    vmem = pltpu.VMEM
    grid_shape = (3, xs + 2, ys + 2 * SUB, lanes)
    tall = (edge, groups, edge + 2 * SUB, lanes)
    flat = (edge, groups, edge, lanes)
    native = (plane // lanes, slots * edge, lanes)
    smem = pl.BlockSpec(memory_space=pltpu.SMEM)
    return pl.pallas_call(
        functools.partial(step_kernel, sizes),
        out_shape=(
            vmem(grid_shape, f32),
            vmem(grid_shape, f32),
            vmem((3, xs, 2, ys, lanes), f32),
            vmem((2, 3, xs, lanes), f32),
            vmem((2, 3, ys, lanes), f32),
            vmem((3,) + flat, f32),
            vmem(native, f32),
            vmem(native, f32),
        ),
        in_specs=[smem, smem, pl.BlockSpec(memory_space=pltpu.HBM), pl.BlockSpec(memory_space=pltpu.HBM)],
        out_specs=(pl.BlockSpec(memory_space=vmem),) * 8,
        scratch_shapes=[
            vmem((2, 3, xs, lanes), f32),
            vmem((2, 3, ys, lanes), f32),
            vmem((2, 2, 3, xs, lanes), f32),
            vmem((2, 3, ys, lanes), f32),
            vmem((3, ys, lanes), f32),
            vmem((3, xs, 2, ys, lanes), f32),
            vmem((2 * lanes, 2 * lanes), bf16),
            vmem((2 * lanes, groups * lanes), bf16),
            vmem((3, groups, xs, ys, lanes), f32),
            vmem(native, f32),
            vmem(tall, f32),
            vmem((edge + 1,) + flat[1:], f32),
            vmem((edge + 4,) + flat[1:], f32),
            vmem(tall, f32),
            vmem(tall, f32),
            vmem((3,) + flat, f32),
            vmem(tall, f32),
            vmem(tall, f32),
            vmem(flat, f32),
            vmem(flat, f32),
            pltpu.SemaphoreType.DMA((3,)),
            pltpu.SemaphoreType.DMA((plane // lanes,)),
            pltpu.SemaphoreType.DMA((2, 6)),
            pltpu.SemaphoreType.DMA((2, 6)),
        ],
        compiler_params=pltpu.CompilerParams(
            collective_id=0, has_side_effects=True, vmem_limit_bytes=36 * MIB
        ),
    )(corners, owner_list, kept(velocity), kept(box_level.reshape(slots * edge, plane)))


def force_kernel(
    corners, vel, pred, near, yrecv, zrecv, force, native_a, native_b,
    o_hbm, set_hbm, ben_hbm,
    o_ref, comb, place, out_sem, small_sem,
):
    _, xs, ys, lanes = o_ref.shape
    grid = Grid(xs, ys, lanes)
    slots = corners.shape[1]
    edge = force.shape[1]
    box = Box(edge, lanes, slots)
    per = box.per
    stores = []
    for h in range(box.halves):
        part_h = pl.ds(h * lanes, lanes)
        stores.append(pltpu.make_async_copy(native_a.at[h], set_hbm.at[:, part_h], small_sem.at[0, h]))
        stores.append(pltpu.make_async_copy(native_b.at[h], ben_hbm.at[:, part_h], small_sem.at[1, h]))
    for copy in stores:
        copy.start()
    grid.combine(zrecv.at[0], zrecv.at[1], comb)

    def second(c, x, y, value):
        o_ref[c, x, pl.ds(y, SUB)] = 0.5 * vel[c, x + 1, pl.ds(SUB + y, SUB)] + value

    grid.fill_rows(pred, yrecv.at[0], yrecv.at[1])
    grid.section(pred, comb, near, 0.5, second)

    wide = iota((edge, lanes), 1)

    offset = iota((edge, lanes), 1) - iota((edge, lanes), 0)
    spots = [(c, i) for c in range(3) for i in range(edge)]

    def turned(n, force_at):
        ax, ay, az = corners[0, n], corners[1, n], corners[2, n]
        turn = lax.rem(az + lanes - n % per * edge, lanes)
        inside = jnp.logical_and(wide >= az, wide < az + edge)
        for at in range(0, len(spots), TURN):
            some = spots[at : at + TURN]
            blocks = [pltpu.roll(force_at(c, i), turn, 1) for c, i in some]
            olds = [o_ref[c, ax + i, pl.ds(ay, edge), :] for c, i in some]
            for (c, i), old, block in zip(some, olds, blocks):
                o_ref[c, ax + i, pl.ds(ay, edge), :] = old + jnp.where(inside, block, 0.0)

    def deposit(t, carry):
        base = t * DEPOSIT
        g = base // per

        def force_at(c, i):
            return force[c, i, g]

        for e in range(2):
            slot = base + e
            mark = ones(offset == corners[2, slot])
            blank = jnp.zeros_like(mark)
            for r in range(per):
                value = jnp.where(slot % per == r, mark, blank)
                for part in range(2):
                    place[pl.ds(part * lanes + r * edge, edge), e * lanes : (e + 1) * lanes] = value
        left = jnp.concatenate([halves(force_at(c, i)) for c, i in spots], axis=0)
        both = jnp.dot(left, place[...], preferred_element_type=f32)
        for e in range(2, DEPOSIT):
            turned(base + e, force_at)
        for e in range(2):
            ax, ay = corners[0, base + e], corners[1, base + e]
            for n, (c, i) in enumerate(spots):
                rows = pl.ds(ay, edge)
                o_ref[c, ax + i, rows, :] = (
                    o_ref[c, ax + i, rows, :]
                    + both[n * edge : (n + 1) * edge, e * lanes : (e + 1) * lanes]
                )
        return carry

    lax.fori_loop(0, slots // DEPOSIT, deposit, 0)
    for c in range(3):
        stores.append(pltpu.make_async_copy(o_ref.at[c], o_hbm.at[c], out_sem.at[c]))
        stores[-1].start()
    for copy in stores:
        copy.wait()


def force_call(shapes, block, corners, handed):
    slots, edge, plane = shapes
    _, xs, ys, lanes = block
    flat = (slots * edge, plane)
    whole = pl.BlockSpec(memory_space=pltpu.VMEM)
    smem = pl.BlockSpec(memory_space=pltpu.SMEM)
    handed = [pltpu.with_memory_space_constraint(a, pltpu.VMEM) for a in handed]
    result, settled, bending = pl.pallas_call(
        force_kernel,
        out_shape=(
            jax.ShapeDtypeStruct(block, f32),
            jax.ShapeDtypeStruct(flat, f32),
            jax.ShapeDtypeStruct(flat, f32),
        ),
        in_specs=[smem] + [whole] * 8,
        out_specs=(pl.BlockSpec(memory_space=pltpu.HBM),) * 3,
        scratch_shapes=[
            pltpu.VMEM(block, f32),
            pltpu.VMEM((3, ys, lanes), f32),
            pltpu.VMEM((2 * lanes, 2 * lanes), bf16),
            pltpu.SemaphoreType.DMA((3,)),
            pltpu.SemaphoreType.DMA((2, plane // lanes)),
        ],
        compiler_params=pltpu.CompilerParams(vmem_limit_bytes=24 * MIB),
    )(corners, *handed)
    return result, settled.reshape(shapes), bending.reshape(shapes)


def local(velocity, box_level, corners, owner_list):
    turned, owner_list = kept(corners.T), kept(owner_list)
    handed = step_call(velocity, box_level, turned, owner_list)
    return force_call(box_level.shape, velocity.shape, turned, handed)


def solution(mesh):
    placed = (
        P(None, "gx", "gy", "gz"),
        P(("gx", "gy", "gz"), None, None),
        P(("gx", "gy", "gz"), None),
        P(("gx", "gy", "gz")),
    )
    return jax.shard_map(
        local,
        mesh=mesh,
        in_specs=placed,
        out_specs=(
            P(None, "gx", "gy", "gz"),
            P(("gx", "gy", "gz"), None, None),
            P(("gx", "gy", "gz"), None, None),
        ),
        check_vma=False,
    )
```

```python
import functools
import math

import jax
import jax.numpy as jnp
from jax import lax
from jax.experimental import pallas as pl
from jax.experimental.pallas import tpu as pltpu
from jax.sharding import PartitionSpec as P

ITERS = 12

box_step = 0.25
pseudo_step = 0.3
weno_floor = 1e-06
band_width = 1.5
tension = 2.0
grid_step = 0.2
viscosity = 0.1
normal_floor = 0.5
speck = 1.1e-19

SUB = 8
PLANES = 6
FUSE = 4
EARLY = 1
DEPOSIT = 4
TURN = 12
MIB = 1 << 20

MESH = pl.DeviceIdType.MESH
f32, bf16 = jnp.float32, jnp.bfloat16


def iota(shape, dim):
    return lax.broadcasted_iota(jnp.int32, shape, dim)


def halves(x):
    high = x.astype(bf16)
    return jnp.concatenate([high, (x - high.astype(f32)).astype(bf16)], axis=1)


def ones(mask):
    return jnp.where(mask, 1.0, 0.0).astype(bf16)


class Box:
    def __init__(self, edge, lanes, slots):
        self.edge, self.lanes = edge, lanes
        self.per = lanes // edge
        self.groups = slots // self.per
        self.halves = edge // SUB
        self.here = pl.ds(SUB, edge)
        self.below = pl.ds(SUB - 1, edge)
        self.above = pl.ds(SUB + 1, edge)
        self.block8 = iota((SUB, lanes), 1) // edge
        self.row8 = iota((SUB, lanes), 0)
        self.block = iota((edge, lanes), 1) // edge
        k_at = iota((edge, lanes), 1) % edge
        self.k_first, self.k_last = k_at == 0, k_at == edge - 1
        self.k_at = k_at

    def prev(self, x, n=1):
        return pltpu.roll(x, n, 1)

    def next(self, x, n=1):
        return pltpu.roll(x, self.lanes - n, 1)

    def swap_blocks(self, x):
        x = pltpu.roll(x, 0, 1, stride=self.edge, stride_axis=0)
        for b in (1, 2, 4):
            x = jnp.where((self.block8 & b) != 0, pltpu.roll(x, SUB - b, 0), x)
        x = pltpu.roll(x, 0, 1, stride=self.edge, stride_axis=0)
        x = pltpu.roll(x, 4, 0)
        for b in (1, 2):
            x = jnp.where((self.row8 & b) != 0, pltpu.roll(x, b, 0), pltpu.roll(x, SUB - b, 0))
        return pltpu.roll(x, 1, 0)

    def put(self, ref, i, g, value):
        last = SUB + self.edge
        ref[i, g, self.here] = value
        ref[i, g, SUB - 1 : SUB] = value[:1]
        ref[i, g, last : last + 1] = value[self.edge - 1 :]


def fetch_levels(box, native, lev, first, count):
    edge, per = box.edge, box.per
    for n in range(count):
        i = first + n
        for g in range(box.groups):
            pieces = [
                box.swap_blocks(native[h, pl.ds(g * per * edge + i, per, stride=edge), :])
                for h in range(box.halves)
            ]
            box.put(lev, i, g, 2.0 * jnp.concatenate(pieces, axis=0))


def window_matrix(box, corners):
    lanes, edge = box.lanes, box.edge
    columns = []
    for g in range(box.groups):
        block = iota((1, lanes), 1) // edge
        first = jnp.zeros((1, lanes), jnp.int32)
        for s in range(box.per):
            first = jnp.where(block == s, corners[2, g * box.per + s], first)
        wanted = first + iota((1, lanes), 1) % edge
        columns.append(ones(iota((lanes, lanes), 0) == wanted))
    both = jnp.concatenate(columns, axis=1)
    return jnp.concatenate([both, both], axis=0)


def shift_matrix(lanes):
    z, l = iota((lanes, lanes), 0), iota((lanes, lanes), 1)
    both = jnp.concatenate([ones(z == l - 1), ones(z == l + 1)], axis=1)
    return jnp.concatenate([both, both], axis=0)


def gather_motion(box, corners, wide, mot):
    edge = box.edge
    slots = box.per * box.groups
    places = [[corners[d, n] for d in range(2)] for n in range(slots)]

    def gather(first, count):
        for n in range(count):
            i = first + n
            for g in range(box.groups):
                for c in range(3):
                    acc = None
                    for s in range(box.per):
                        ax, ay = places[g * box.per + s]
                        rows = wide[c, g, ax + i, pl.ds(ay, edge), :]
                        acc = rows if acc is None else jnp.where(box.block == s, rows, acc)
                    mot[c, i, g] = acc

    return gather


def lean(e1, e2, e3, e4):
    floor = 3.0 * weno_floor
    s2, s3 = e2 * e2, e3 * e3
    b1 = e1 * (e1 - 2.75 * e2) + (2.5 * s2 + floor)
    b2 = e2 * (e2 - 1.25 * e3) + (s3 + floor)
    b3 = e4 * (e4 - 2.75 * e3) + (2.5 * s3 + floor)
    a1, a2, a3 = 3.0 * (b1 * b1), b2 * b2, b3 * b3
    t = 2.0 * e3
    p = a2 * a3
    top = p * (e1 - 2.5 * e2) + a1 * (a2 * (0.5 * e4 - t) - a3 * (e2 + t))
    return top, p + a1 * (a2 + 2.0 * a3)


def advect_levels(box, lev, mi, di, mj, dj, mot, psa, sign, rate):
    edge, here, below, above = box.edge, box.here, box.below, box.above
    zero = jnp.zeros((edge, box.lanes), f32)
    last = SUB + edge

    for g in range(box.groups):
        mi[0, g] = zero
        for n in (0, 1, edge + 1, edge + 2, edge + 3):
            di[n, g] = zero

    def rise(i, carry):
        for g in range(box.groups):
            @pl.when(i > 0)
            def _(g=g):
                mi[i, g] = lev[i, g, here] - lev[i - 1, g, here]

            step = lev[i, g, here] - lev[i, g, below]
            mj[i, g, here] = step
            mj[i, g, last : last + 1] = step[edge - 1 :]
        return carry

    lax.fori_loop(0, edge, rise, 0, unroll=True)
    for g in range(box.groups):
        mi[edge, g] = mi[edge - 1, g]

    def bow(i, carry):
        for g in range(box.groups):
            if_last = mi[i, g] - mi[i + 1, g]
            di[i + 2, g] = if_last
            dj[i, g, pl.ds(0, SUB)] = zero[:SUB]
            dj[i, g, pl.ds(last, SUB)] = zero[:SUB]
            dj[i, g, here] = mj[i, g, here] - mj[i, g, above]
        return carry

    lax.fori_loop(0, edge, bow, 0, unroll=4)

    k_low2 = box.k_at >= 2
    k_up1 = box.k_at < edge - 1
    k_up2 = box.k_at < edge - 2

    def advect(i, carry):
        for g in range(box.groups):
            level = lev[i, g, here]
            drift = turn = None
            for d in range(3):
                if d == 0:
                    m0, m1 = mi[i, g], mi[i + 1, g]
                    ds = [di[i + n, g] for n in range(5)]
                elif d == 1:
                    m0, m1 = mj[i, g, here], mj[i, g, above]
                    ds = [dj[i, g, pl.ds(SUB - 2 + n, edge)] for n in range(5)]
                else:
                    m0 = jnp.where(box.k_first, 0.0, level - box.prev(level))
                    m1 = jnp.where(box.k_last, m0, box.next(m0))
                    mid = m0 - m1
                    ds = [
                        jnp.where(k_low2, box.prev(mid, 2), 0.0),
                        box.prev(mid, 1),
                        mid,
                        jnp.where(k_up1, box.next(mid, 1), 0.0),
                        jnp.where(k_up2, box.next(mid, 2), 0.0),
                    ]
                speed = mot[d, i, g]
                pos = speed > 0.0
                e1 = jnp.where(pos, ds[0], ds[4])
                e2 = jnp.where(pos, ds[1], ds[3])
                e4 = jnp.where(pos, ds[3], ds[1])
                top, bottom = lean(e1, e2, ds[2], e4)
                part = speed * jnp.where(pos, m0, m1)
                extra = jnp.abs(speed) * (top / bottom)
                drift = part if drift is None else drift + part
                turn = extra if turn is None else turn + extra
            out = 0.5 * level - (0.5 * box_step) * drift - (box_step / 6.0) * turn
            box.put(psa, i, g, out)
            sign[i, g] = jnp.where(out > 0.0, 1.0, -1.0)
            rate[i, g] = pseudo_step * out * lax.rsqrt(out * out + 1.0)
        return carry

    lax.fori_loop(0, edge, advect, 0, unroll=8)


def reinitialize(box, psa, psb, sign, rate):
    edge, here, below, above = box.edge, box.here, box.below, box.above
    low = jnp.where(box.k_first, 0.0, 1.0)
    high = jnp.where(box.k_last, 0.0, 1.0)

    def sweep(src, dst):
        for i in range(edge):
            for g in range(box.groups):
                cur = src[i, g, here]
                s, r = sign[i, g], rate[i, g]
                signed = s * cur
                x = signed - jnp.minimum(
                    s * src[max(i - 1, 0), g, here], s * src[min(i + 1, edge - 1), g, here]
                )
                y = signed - jnp.minimum(s * src[i, g, below], s * src[i, g, above])
                z = jnp.maximum(
                    (s * low) * (cur - box.prev(cur)), (s * high) * (cur - box.next(cur))
                )
                x = jnp.maximum(x, speck)
                y, z = jnp.maximum(y, 0.0), jnp.maximum(z, 0.0)
                total = x * x + y * y + z * z
                box.put(dst, i, g, (cur + r) - r * (total * lax.rsqrt(total)))

    def two_sweeps(n, carry):
        sweep(psa, psb)
        sweep(psb, psa)
        return carry

    def run(pairs):
        if pairs == 1:
            two_sweeps(0, 0)
        else:
            lax.fori_loop(0, pairs, two_sweeps, 0)

    return run


def curve_levels(box, owners, psi, nx, ny, part, force, native_a, native_b):
    edge, per, here, below, above = box.edge, box.per, box.here, box.below, box.above

    def spread(x):
        return jnp.where(box.k_last, x, box.next(x)) - jnp.where(box.k_first, x, box.prev(x))

    def bend(i, carry):
        for g in range(box.groups):
            cur = psi[i, g, here]
            c0 = psi[jnp.minimum(i + 1, edge - 1), g, here] - psi[jnp.maximum(i - 1, 0), g, here]
            c1 = psi[i, g, above] - psi[i, g, below]
            c2 = spread(cur)
            floor = 4.0 * normal_floor * normal_floor
            inverse = lax.rsqrt(jnp.maximum(c0 * c0 + c1 * c1 + c2 * c2, floor))
            nx[i, g] = c0 * inverse
            box.put(ny, i, g, c1 * inverse)
            part[i, g] = spread(c2 * inverse)
            for d, c in enumerate((c0, c1, c2)):
                force[d, i, g] = c
        return carry

    lax.fori_loop(0, edge, bend, 0, unroll=8)

    alive = []
    for g in range(box.groups):
        live = jnp.zeros((edge, box.lanes), f32)
        for s in range(per):
            on = jnp.where(owners[g * per + s] >= 0, 1.0, 0.0)
            live = jnp.where(box.block == s, on, live)
        alive.append(live)

    def push(i, carry):
        for g in range(box.groups):
            live = alive[g]
            level = psi[i, g, here] * live
            ends = nx[jnp.minimum(i + 1, edge - 1), g] - nx[jnp.maximum(i - 1, 0), g]
            curve = (0.5 * live) * (ends + (ny[i, g, above] - ny[i, g, below]) + part[i, g])
            for h in range(box.halves):
                at = pl.ds(g * per * edge + i, per, stride=edge)
                rows = slice(h * SUB, (h + 1) * SUB)
                native_a[h, at, :] = box.swap_blocks(level[rows])
                native_b[h, at, :] = box.swap_blocks(curve[rows])
            ratio = level * (1.0 / band_width)
            scale = 0.5 * grid_step * tension / (band_width * math.sqrt(math.pi))
            strength = scale * curve * jnp.exp(-(ratio * ratio)) * live
            for d in range(3):
                force[d, i, g] = force[d, i, g] * strength
        return carry

    lax.fori_loop(0, edge, push, 0, unroll=8)


class Grid:
    def __init__(self, xs, ys, lanes):
        self.xs, self.ys, self.lanes = xs, ys, lanes
        self.here = pl.ds(SUB, ys)
        self.below = pl.ds(SUB - 1, ys)
        self.above = pl.ds(SUB + 1, ys)
        self.rows = ys + 2 * SUB
        self.shape = (3, xs + 2, self.rows, lanes)
        self.lane = iota((ys, lanes), 1)

    def row_of(self, ref, c, x, row):
        flat = ref.reshape(3 * (self.xs + 2) * self.rows, self.lanes)
        return flat.at[pl.ds((c * (self.xs + 2) + x) * self.rows + row, SUB, stride=self.rows), :]

    def fill_rows(self, ref, low, high):
        for c in range(3):
            for x in range(0, self.xs, SUB):
                part = pl.ds(x, SUB)
                self.row_of(ref, c, x + 1, SUB - 1)[...] = low[c, part]
                self.row_of(ref, c, x + 1, SUB + self.ys)[...] = high[c, part]

    def take_rows(self, ref, ysend):
        for c in range(3):
            for x in range(0, self.xs, SUB):
                part = pl.ds(x, SUB)
                ysend[0, c, part] = self.row_of(ref, c, x + 1, SUB + self.ys - 1)[...]
                ysend[1, c, part] = self.row_of(ref, c, x + 1, SUB)[...]

    def combine(self, zlow, zhigh, comb):
        high = pltpu.roll(zhigh[...], self.lanes - 2, 1)
        for c in range(3):
            comb[c] = jnp.where(self.lane % 4 == c, zlow[...], high)

    def pack(self, value, c, x, faces):
        lane = self.lane[: value.shape[0]] - 4 * x
        turned = pltpu.roll(value, 4 * x + c + 1, 1)
        return jnp.where(lane == c, turned, faces[0]), jnp.where(lane == c + 1, turned, faces[1])

    def shift(self, src, shifts, near, pieces, also):
        span = self.xs // pieces

        def part(t, carry):
            left = [halves(src[c, 1 + span * t + n, self.here]) for c in range(3) for n in range(span)]
            both = jnp.dot(jnp.concatenate(left, axis=0), shifts[...], preferred_element_type=f32)
            for c in range(3):
                for n in range(span):
                    at = (c * span + n) * self.ys
                    for e in range(2):
                        near[c, span * t + n, e] = both[at : at + self.ys, e * self.lanes : (e + 1) * self.lanes]
            also(t)
            return carry

        lax.fori_loop(0, pieces, part, 0)

    def section(self, src, comb, near, scale, emit, ends_done, unroll):
        h = scale * grid_step * viscosity
        lane = self.lane[:SUB]
        first, last = lane == 0, lane == self.lanes - 1

        def plane(x, carry):
            for y in range(0, self.ys, SUB):
                rows, tile = pl.ds(SUB + y, SUB), pl.ds(y, SUB)
                centre = [src[c, x + 1, rows] for c in range(3)]
                w = [(0.5 * scale * grid_step) * v for v in centre]
                up, down = [h - v for v in w], [h + v for v in w]
                rim = jnp.where(first, down[2], jnp.where(last, up[2], 0.0))
                values = []
                for c in range(3):
                    turn = lax.rem(2 * self.lanes - c - 4 * x, self.lanes)
                    halo = pltpu.roll(comb[c, tile], turn, 1)
                    values.append(
                        (scale - 6.0 * h) * centre[c]
                        + up[0] * src[c, x + 2, rows]
                        + down[0] * src[c, x, rows]
                        + up[1] * src[c, x + 1, pl.ds(SUB + y + 1, SUB)]
                        + down[1] * src[c, x + 1, pl.ds(SUB + y - 1, SUB)]
                        + up[2] * near[c, x, 1, tile]
                        + down[2] * near[c, x, 0, tile]
                        + rim * halo
                    )
                emit(x, y, values)
            return carry

        if ends_done is None:
            lax.fori_loop(0, self.xs, plane, 0, unroll=unroll)
            return
        plane(0, 0)
        plane(self.xs - 1, 0)
        ends_done()
        lax.fori_loop(1, self.xs - 1, plane, 0, unroll=unroll)


def step_kernel(
    sizes, corners, owners, v_hbm, lev_hbm,
    vel, pred, near1, yrecv1, zrecv1, force, native_a, native_b,
    yrecv0, zrecv0, ysend, zsend, comb, near0, shifts, windows, wide,
    native, lev, mi, di, mj, dj, mot, psa, psb, sign, rate,
    local_sem, lev_sem, send_sem, recv_sem,
):
    _, xs, ys, lanes = v_hbm.shape
    grid = Grid(xs, ys, lanes)
    slots = corners.shape[1]
    edge = lev.shape[0]
    box = Box(edge, lanes, slots)
    inner = pl.ds(1, xs)
    loads = [
        pltpu.make_async_copy(v_hbm.at[c], vel.at[c, inner, grid.here], local_sem.at[c]) for c in range(3)
    ]
    levels = [
        pltpu.make_async_copy(lev_hbm.at[:, pl.ds(h * lanes, lanes)], native.at[h], lev_sem.at[h])
        for h in range(box.halves)
    ]
    for part in loads + levels:
        part.start()
    ups, downs = [], []
    for axis in ("gx", "gy", "gz"):
        me, n = lax.axis_index(axis), sizes[axis]
        ups.append({axis: lax.rem(me + 1, n)})
        downs.append({axis: lax.rem(me + n - 1, n)})
    barrier = pltpu.get_barrier_semaphore()
    for target in ups + downs:
        pl.semaphore_signal(barrier, inc=1, device_id=target, device_id_type=MESH)
    shifts[...] = shift_matrix(lanes)
    windows[...] = window_matrix(box, corners)

    copies = [[], []]

    def send(r, n, src, dst, target):
        copy = pltpu.make_async_remote_copy(
            src_ref=src,
            dst_ref=dst,
            send_sem=send_sem.at[r, n],
            recv_sem=recv_sem.at[r, n],
            device_id=target,
            device_id_type=MESH,
        )
        copy.start()
        copies[r].append(copy)

    def send_x(r, src):
        send(r, 0, src.at[:, xs, grid.here], src.at[:, 0, grid.here], ups[0])
        send(r, 1, src.at[:, 1, grid.here], src.at[:, xs + 1, grid.here], downs[0])

    def send_yz(r, yrecv, zrecv):
        send(r, 2, ysend.at[r, 0], yrecv.at[0], ups[1])
        send(r, 3, ysend.at[r, 1], yrecv.at[1], downs[1])
        send(r, 4, zsend.at[r, 0], zrecv.at[0], ups[2])
        send(r, 5, zsend.at[r, 1], zrecv.at[1], downs[2])

    blank = jnp.zeros((ys, lanes), f32)
    faces = blank, blank
    for c in range(3):
        loads[c].wait()

        def pack(x, faces, c=c):
            return grid.pack(vel[c, x + 1, grid.here], c, x, faces)

        faces = lax.fori_loop(0, xs, pack, faces, unroll=8)
    zsend[0, 0], zsend[0, 1] = faces
    zsend[1, 0], zsend[1, 1] = blank, blank
    grid.take_rows(vel, ysend.at[0])
    pl.semaphore_wait(barrier, 6)
    send_x(0, vel)
    send_yz(0, yrecv0, zrecv0)
    for part in levels:
        part.wait()
    span = xs // 2

    def spread(t, carry):
        left = [halves(vel[c, span * t + n + 1, grid.here]) for c in range(3) for n in range(span)]
        both = jnp.dot(jnp.concatenate(left, axis=0), windows[...], preferred_element_type=f32)
        for c in range(3):
            for n in range(span):
                at = (c * span + n) * ys
                for g in range(box.groups):
                    wide[c, g, span * t + n] = both[at : at + ys, g * lanes : (g + 1) * lanes]
        fetch_levels(box, native, lev, t * (edge // 2), edge // 2)
        return carry

    lax.fori_loop(0, 2, spread, 0)
    gather = gather_motion(box, corners, wide, mot)
    grid.shift(vel, shifts, near0, 2, lambda t: gather(t * (edge // 2), edge // 2))
    advect_levels(box, lev, mi, di, mj, dj, mot, psa, sign, rate)
    reinitialize(box, psa, psb, sign, rate)(EARLY)
    for copy in copies[0]:
        copy.wait()
    grid.fill_rows(vel, yrecv0.at[0], yrecv0.at[1])
    grid.combine(zrecv0.at[0], zrecv0.at[1], comb)

    def first(x, y, values):
        tile = pl.ds(y, SUB)
        faces = zsend[1, 0, tile], zsend[1, 1, tile]
        for c, value in enumerate(values):
            pred[c, x + 1, pl.ds(SUB + y, SUB)] = value
            faces = grid.pack(value, c, x, faces)
        zsend[1, 0, tile], zsend[1, 1, tile] = faces

    grid.section(vel, comb, near0, 1.0, first, lambda: send_x(1, pred), PLANES)
    grid.take_rows(pred, ysend.at[1])
    send_yz(1, yrecv1, zrecv1)
    two_sweeps = reinitialize(box, psa, psb, sign, rate)
    if FUSE:
        grid.shift(pred, shifts, near1, FUSE, lambda t: two_sweeps(1))
    else:
        grid.shift(pred, shifts, near1, 2, lambda t: None)
    two_sweeps(ITERS // 2 - EARLY - FUSE)
    curve_levels(box, owners, psa, mi, mj, di, force, native_a, native_b)
    for copy in copies[1]:
        copy.wait()


def kept(x):
    return pltpu.with_memory_space_constraint(x, pltpu.HBM)


def step_call(velocity, box_level, corners, owner_list):
    sizes = {axis: lax.axis_size(axis) for axis in ("gx", "gy", "gz")}
    _, xs, ys, lanes = velocity.shape
    slots, edge, plane = box_level.shape
    groups = slots * edge // lanes
    vmem = pltpu.VMEM
    grid_shape = (3, xs + 2, ys + 2 * SUB, lanes)
    tall = (edge, groups, edge + 2 * SUB, lanes)
    flat = (edge, groups, edge, lanes)
    native = (plane // lanes, slots * edge, lanes)
    smem = pl.BlockSpec(memory_space=pltpu.SMEM)
    return pl.pallas_call(
        functools.partial(step_kernel, sizes),
        out_shape=(
            vmem(grid_shape, f32),
            vmem(grid_shape, f32),
            vmem((3, xs, 2, ys, lanes), f32),
            vmem((2, 3, xs, lanes), f32),
            vmem((2, ys, lanes), f32),
            vmem((3,) + flat, f32),
            vmem(native, f32),
            vmem(native, f32),
        ),
        in_specs=[smem, smem, pl.BlockSpec(memory_space=pltpu.HBM), pl.BlockSpec(memory_space=pltpu.HBM)],
        out_specs=(pl.BlockSpec(memory_space=vmem),) * 8,
        scratch_shapes=[
            vmem((2, 3, xs, lanes), f32),
            vmem((2, ys, lanes), f32),
            vmem((2, 2, 3, xs, lanes), f32),
            vmem((2, 2, ys, lanes), f32),
            vmem((3, ys, lanes), f32),
            vmem((3, xs, 2, ys, lanes), f32),
            vmem((2 * lanes, 2 * lanes), bf16),
            vmem((2 * lanes, groups * lanes), bf16),
            vmem((3, groups, xs, ys, lanes), f32),
            vmem(native, f32),
            vmem(tall, f32),
            vmem((edge + 1,) + flat[1:], f32),
            vmem((edge + 4,) + flat[1:], f32),
            vmem(tall, f32),
            vmem(tall, f32),
            vmem((3,) + flat, f32),
            vmem(tall, f32),
            vmem(tall, f32),
            vmem(flat, f32),
            vmem(flat, f32),
            pltpu.SemaphoreType.DMA((3,)),
            pltpu.SemaphoreType.DMA((plane // lanes,)),
            pltpu.SemaphoreType.DMA((2, 6)),
            pltpu.SemaphoreType.DMA((2, 6)),
        ],
        compiler_params=pltpu.CompilerParams(
            collective_id=0, has_side_effects=True, vmem_limit_bytes=36 * MIB
        ),
    )(corners, owner_list, kept(velocity), kept(box_level.reshape(slots * edge, plane)))


def force_kernel(
    corners, vel, pred, near, yrecv, zrecv, force, native_a, native_b,
    o_hbm, set_hbm, ben_hbm,
    o_ref, comb, place, out_sem, small_sem,
):
    _, xs, ys, lanes = o_ref.shape
    grid = Grid(xs, ys, lanes)
    slots = corners.shape[1]
    edge = force.shape[1]
    box = Box(edge, lanes, slots)
    per = box.per
    stores = []
    for h in range(box.halves):
        part_h = pl.ds(h * lanes, lanes)
        stores.append(pltpu.make_async_copy(native_a.at[h], set_hbm.at[:, part_h], small_sem.at[0, h]))
        stores.append(pltpu.make_async_copy(native_b.at[h], ben_hbm.at[:, part_h], small_sem.at[1, h]))
    for copy in stores:
        copy.start()
    grid.combine(zrecv.at[0], zrecv.at[1], comb)

    def second(x, y, values):
        for c, value in enumerate(values):
            o_ref[c, x, pl.ds(y, SUB)] = 0.5 * vel[c, x + 1, pl.ds(SUB + y, SUB)] + value

    grid.fill_rows(pred, yrecv.at[0], yrecv.at[1])
    grid.section(pred, comb, near, 0.5, second, None, 8)

    wide = iota((edge, lanes), 1)

    offset = iota((edge, lanes), 1) - iota((edge, lanes), 0)
    spots = [(c, i) for c in range(3) for i in range(edge)]

    def turned(n, force_at):
        ax, ay, az = corners[0, n], corners[1, n], corners[2, n]
        turn = lax.rem(az + lanes - n % per * edge, lanes)
        inside = jnp.logical_and(wide >= az, wide < az + edge)
        for at in range(0, len(spots), TURN):
            some = spots[at : at + TURN]
            blocks = [pltpu.roll(force_at(c, i), turn, 1) for c, i in some]
            olds = [o_ref[c, ax + i, pl.ds(ay, edge), :] for c, i in some]
            for (c, i), old, block in zip(some, olds, blocks):
                o_ref[c, ax + i, pl.ds(ay, edge), :] = old + jnp.where(inside, block, 0.0)

    def deposit(t, carry):
        base = t * DEPOSIT
        g = base // per

        def force_at(c, i):
            return force[c, i, g]

        for e in range(2):
            slot = base + e
            mark = ones(offset == corners[2, slot])
            blank = jnp.zeros_like(mark)
            for r in range(per):
                value = jnp.where(slot % per == r, mark, blank)
                for part in range(2):
                    place[pl.ds(part * lanes + r * edge, edge), e * lanes : (e + 1) * lanes] = value
        left = jnp.concatenate([halves(force_at(c, i)) for c, i in spots], axis=0)
        both = jnp.dot(left, place[...], preferred_element_type=f32)
        for e in range(2, DEPOSIT):
            turned(base + e, force_at)
        for e in range(2):
            ax, ay = corners[0, base + e], corners[1, base + e]
            for n, (c, i) in enumerate(spots):
                rows = pl.ds(ay, edge)
                o_ref[c, ax + i, rows, :] = (
                    o_ref[c, ax + i, rows, :]
                    + both[n * edge : (n + 1) * edge, e * lanes : (e + 1) * lanes]
                )
        return carry

    lax.fori_loop(0, slots // DEPOSIT, deposit, 0)
    for c in range(3):
        stores.append(pltpu.make_async_copy(o_ref.at[c], o_hbm.at[c], out_sem.at[c]))
        stores[-1].start()
    for copy in stores:
        copy.wait()


def force_call(shapes, block, corners, handed):
    slots, edge, plane = shapes
    _, xs, ys, lanes = block
    flat = (slots * edge, plane)
    whole = pl.BlockSpec(memory_space=pltpu.VMEM)
    smem = pl.BlockSpec(memory_space=pltpu.SMEM)
    handed = [pltpu.with_memory_space_constraint(a, pltpu.VMEM) for a in handed]
    result, settled, bending = pl.pallas_call(
        force_kernel,
        out_shape=(
            jax.ShapeDtypeStruct(block, f32),
            jax.ShapeDtypeStruct(flat, f32),
            jax.ShapeDtypeStruct(flat, f32),
        ),
        in_specs=[smem] + [whole] * 8,
        out_specs=(pl.BlockSpec(memory_space=pltpu.HBM),) * 3,
        scratch_shapes=[
            pltpu.VMEM(block, f32),
            pltpu.VMEM((3, ys, lanes), f32),
            pltpu.VMEM((2 * lanes, 2 * lanes), bf16),
            pltpu.SemaphoreType.DMA((3,)),
            pltpu.SemaphoreType.DMA((2, plane // lanes)),
        ],
        compiler_params=pltpu.CompilerParams(vmem_limit_bytes=24 * MIB),
    )(corners, *handed)
    return result, settled.reshape(shapes), bending.reshape(shapes)


def local(velocity, box_level, corners, owner_list):
    turned, owner_list = kept(corners.T), kept(owner_list)
    handed = step_call(velocity, box_level, turned, owner_list)
    return force_call(box_level.shape, velocity.shape, turned, handed)


def solution(mesh):
    placed = (
        P(None, "gx", "gy", "gz"),
        P(("gx", "gy", "gz"), None, None),
        P(("gx", "gy", "gz"), None),
        P(("gx", "gy", "gz")),
    )
    return jax.shard_map(
        local,
        mesh=mesh,
        in_specs=placed,
        out_specs=(
            P(None, "gx", "gy", "gz"),
            P(("gx", "gy", "gz"), None, None),
            P(("gx", "gy", "gz"), None, None),
        ),
        check_vma=False,
    )
```

```python
import functools
import math

import jax
import jax.numpy as jnp
from jax import lax
from jax.experimental import pallas as pl
from jax.experimental.pallas import tpu as pltpu
from jax.sharding import PartitionSpec as P

ITERS = 12

box_step = 0.25
pseudo_step = 0.3
weno_floor = 1e-06
band_width = 1.5
tension = 2.0
grid_step = 0.2
viscosity = 0.1
normal_floor = 0.5
speck = 1.1e-19

SUB = 8
PLANES = 6
FUSE = 2
AHEAD = (1, 2, 3)
DEPOSIT = 4
TURN = 12
MIB = 1 << 20

MESH = pl.DeviceIdType.MESH
f32, bf16 = jnp.float32, jnp.bfloat16


def iota(shape, dim):
    return lax.broadcasted_iota(jnp.int32, shape, dim)


def halves(x):
    high = x.astype(bf16)
    return jnp.concatenate([high, (x - high.astype(f32)).astype(bf16)], axis=1)


def ones(mask):
    return jnp.where(mask, 1.0, 0.0).astype(bf16)


class Box:
    def __init__(self, edge, lanes, slots):
        self.edge, self.lanes = edge, lanes
        self.per = lanes // edge
        self.groups = slots // self.per
        self.halves = edge // SUB
        self.here = pl.ds(SUB, edge)
        self.below = pl.ds(SUB - 1, edge)
        self.above = pl.ds(SUB + 1, edge)
        self.block8 = iota((SUB, lanes), 1) // edge
        self.row8 = iota((SUB, lanes), 0)
        self.block = iota((edge, lanes), 1) // edge
        k_at = iota((edge, lanes), 1) % edge
        self.k_first, self.k_last = k_at == 0, k_at == edge - 1
        self.k_at = k_at

    def prev(self, x, n=1):
        return pltpu.roll(x, n, 1)

    def next(self, x, n=1):
        return pltpu.roll(x, self.lanes - n, 1)

    def swap_blocks(self, x):
        x = pltpu.roll(x, 0, 1, stride=self.edge, stride_axis=0)
        for b in (1, 2, 4):
            x = jnp.where((self.block8 & b) != 0, pltpu.roll(x, SUB - b, 0), x)
        x = pltpu.roll(x, 0, 1, stride=self.edge, stride_axis=0)
        x = pltpu.roll(x, 4, 0)
        for b in (1, 2):
            x = jnp.where((self.row8 & b) != 0, pltpu.roll(x, b, 0), pltpu.roll(x, SUB - b, 0))
        return pltpu.roll(x, 1, 0)

    def put(self, ref, i, g, value):
        last = SUB + self.edge
        ref[i, g, self.here] = value
        ref[i, g, SUB - 1 : SUB] = value[:1]
        ref[i, g, last : last + 1] = value[self.edge - 1 :]


def fetch_levels(box, native, lev, first, count):
    edge, per = box.edge, box.per
    for n in range(count):
        i = first + n
        for g in range(box.groups):
            pieces = [
                box.swap_blocks(native[h, pl.ds(g * per * edge + i, per, stride=edge), :])
                for h in range(box.halves)
            ]
            box.put(lev, i, g, 2.0 * jnp.concatenate(pieces, axis=0))


def window_matrix(box, corners):
    lanes, edge = box.lanes, box.edge
    columns = []
    for g in range(box.groups):
        block = iota((1, lanes), 1) // edge
        first = jnp.zeros((1, lanes), jnp.int32)
        for s in range(box.per):
            first = jnp.where(block == s, corners[2, g * box.per + s], first)
        wanted = first + iota((1, lanes), 1) % edge
        columns.append(ones(iota((lanes, lanes), 0) == wanted))
    both = jnp.concatenate(columns, axis=1)
    return jnp.concatenate([both, both], axis=0)


def shift_matrix(lanes):
    z, l = iota((lanes, lanes), 0), iota((lanes, lanes), 1)
    both = jnp.concatenate([ones(z == l - 1), ones(z == l + 1)], axis=1)
    return jnp.concatenate([both, both], axis=0)


def gather_motion(box, corners, wide, mot):
    edge = box.edge
    slots = box.per * box.groups
    places = [[corners[d, n] for d in range(2)] for n in range(slots)]

    def gather(first, count):
        for n in range(count):
            i = first + n
            for g in range(box.groups):
                for c in range(3):
                    acc = None
                    for s in range(box.per):
                        ax, ay = places[g * box.per + s]
                        rows = wide[c, g, ax + i, pl.ds(ay, edge), :]
                        acc = rows if acc is None else jnp.where(box.block == s, rows, acc)
                    mot[c, i, g] = acc

    return gather


def lean(e1, e2, e3, e4):
    floor = 3.0 * weno_floor
    s2, s3 = e2 * e2, e3 * e3
    b1 = e1 * (e1 - 2.75 * e2) + (2.5 * s2 + floor)
    b2 = e2 * (e2 - 1.25 * e3) + (s3 + floor)
    b3 = e4 * (e4 - 2.75 * e3) + (2.5 * s3 + floor)
    a1, a2, a3 = 3.0 * (b1 * b1), b2 * b2, b3 * b3
    t = 2.0 * e3
    p = a2 * a3
    top = p * (e1 - 2.5 * e2) + a1 * (a2 * (0.5 * e4 - t) - a3 * (e2 + t))
    return top, p + a1 * (a2 + 2.0 * a3)


def advect_levels(box, lev, mi, di, mj, dj, mot, psa, sign, rate):
    edge, here, below, above = box.edge, box.here, box.below, box.above
    zero = jnp.zeros((edge, box.lanes), f32)
    last = SUB + edge

    for g in range(box.groups):
        mi[0, g] = zero
        for n in (0, 1, edge + 1, edge + 2, edge + 3):
            di[n, g] = zero

    def rise(i, carry):
        for g in range(box.groups):
            @pl.when(i > 0)
            def _(g=g):
                mi[i, g] = lev[i, g, here] - lev[i - 1, g, here]

            step = lev[i, g, here] - lev[i, g, below]
            mj[i, g, here] = step
            mj[i, g, last : last + 1] = step[edge - 1 :]
        return carry

    lax.fori_loop(0, edge, rise, 0, unroll=True)
    for g in range(box.groups):
        mi[edge, g] = mi[edge - 1, g]

    def bow(i, carry):
        for g in range(box.groups):
            if_last = mi[i, g] - mi[i + 1, g]
            di[i + 2, g] = if_last
            dj[i, g, pl.ds(0, SUB)] = zero[:SUB]
            dj[i, g, pl.ds(last, SUB)] = zero[:SUB]
            dj[i, g, here] = mj[i, g, here] - mj[i, g, above]
        return carry

    lax.fori_loop(0, edge, bow, 0, unroll=4)

    k_low2 = box.k_at >= 2
    k_up1 = box.k_at < edge - 1
    k_up2 = box.k_at < edge - 2

    def advect(i, carry):
        for g in range(box.groups):
            level = lev[i, g, here]
            drift = turn = None
            for d in range(3):
                if d == 0:
                    m0, m1 = mi[i, g], mi[i + 1, g]
                    ds = [di[i + n, g] for n in range(5)]
                elif d == 1:
                    m0, m1 = mj[i, g, here], mj[i, g, above]
                    ds = [dj[i, g, pl.ds(SUB - 2 + n, edge)] for n in range(5)]
                else:
                    m0 = jnp.where(box.k_first, 0.0, level - box.prev(level))
                    m1 = jnp.where(box.k_last, m0, box.next(m0))
                    mid = m0 - m1
                    ds = [
                        jnp.where(k_low2, box.prev(mid, 2), 0.0),
                        box.prev(mid, 1),
                        mid,
                        jnp.where(k_up1, box.next(mid, 1), 0.0),
                        jnp.where(k_up2, box.next(mid, 2), 0.0),
                    ]
                speed = mot[d, i, g]
                pos = speed > 0.0
                e1 = jnp.where(pos, ds[0], ds[4])
                e2 = jnp.where(pos, ds[1], ds[3])
                e4 = jnp.where(pos, ds[3], ds[1])
                top, bottom = lean(e1, e2, ds[2], e4)
                part = speed * jnp.where(pos, m0, m1)
                extra = jnp.abs(speed) * (top / bottom)
                drift = part if drift is None else drift + part
                turn = extra if turn is None else turn + extra
            out = 0.5 * level - (0.5 * box_step) * drift - (box_step / 6.0) * turn
            box.put(psa, i, g, out)
            sign[i, g] = jnp.where(out > 0.0, 1.0, -1.0)
            rate[i, g] = pseudo_step * out * lax.rsqrt(out * out + 1.0)
        return carry

    lax.fori_loop(0, edge, advect, 0, unroll=8)


def reinitialize(box, psa, psb, sign, rate):
    edge, here, below, above = box.edge, box.here, box.below, box.above
    low = jnp.where(box.k_first, 0.0, 1.0)
    high = jnp.where(box.k_last, 0.0, 1.0)

    def sweep(src, dst):
        for i in range(edge):
            for g in range(box.groups):
                cur = src[i, g, here]
                s, r = sign[i, g], rate[i, g]
                signed = s * cur
                x = signed - jnp.minimum(
                    s * src[max(i - 1, 0), g, here], s * src[min(i + 1, edge - 1), g, here]
                )
                y = signed - jnp.minimum(s * src[i, g, below], s * src[i, g, above])
                z = jnp.maximum(
                    (s * low) * (cur - box.prev(cur)), (s * high) * (cur - box.next(cur))
                )
                x = jnp.maximum(x, speck)
                y, z = jnp.maximum(y, 0.0), jnp.maximum(z, 0.0)
                total = x * x + y * y + z * z
                box.put(dst, i, g, (cur + r) - r * (total * lax.rsqrt(total)))

    def two_sweeps(n, carry):
        sweep(psa, psb)
        sweep(psb, psa)
        return carry

    def run(pairs):
        if isinstance(pairs, int) and pairs == 1:
            two_sweeps(0, 0)
        else:
            lax.fori_loop(0, pairs, two_sweeps, 0)

    return run


def curve_levels(box, owners, psi, nx, ny, part, force, native_a, native_b):
    edge, per, here, below, above = box.edge, box.per, box.here, box.below, box.above

    def spread(x):
        return jnp.where(box.k_last, x, box.next(x)) - jnp.where(box.k_first, x, box.prev(x))

    def bend(i, carry):
        for g in range(box.groups):
            cur = psi[i, g, here]
            c0 = psi[jnp.minimum(i + 1, edge - 1), g, here] - psi[jnp.maximum(i - 1, 0), g, here]
            c1 = psi[i, g, above] - psi[i, g, below]
            c2 = spread(cur)
            floor = 4.0 * normal_floor * normal_floor
            inverse = lax.rsqrt(jnp.maximum(c0 * c0 + c1 * c1 + c2 * c2, floor))
            nx[i, g] = c0 * inverse
            box.put(ny, i, g, c1 * inverse)
            part[i, g] = spread(c2 * inverse)
            for d, c in enumerate((c0, c1, c2)):
                force[d, i, g] = c
        return carry

    lax.fori_loop(0, edge, bend, 0, unroll=8)

    alive = []
    for g in range(box.groups):
        live = jnp.zeros((edge, box.lanes), f32)
        for s in range(per):
            on = jnp.where(owners[g * per + s] >= 0, 1.0, 0.0)
            live = jnp.where(box.block == s, on, live)
        alive.append(live)

    def push(i, carry):
        for g in range(box.groups):
            live = alive[g]
            level = psi[i, g, here] * live
            ends = nx[jnp.minimum(i + 1, edge - 1), g] - nx[jnp.maximum(i - 1, 0), g]
            curve = (0.5 * live) * (ends + (ny[i, g, above] - ny[i, g, below]) + part[i, g])
            for h in range(box.halves):
                at = pl.ds(g * per * edge + i, per, stride=edge)
                rows = slice(h * SUB, (h + 1) * SUB)
                native_a[h, at, :] = box.swap_blocks(level[rows])
                native_b[h, at, :] = box.swap_blocks(curve[rows])
            ratio = level * (1.0 / band_width)
            scale = 0.5 * grid_step * tension / (band_width * math.sqrt(math.pi))
            strength = scale * curve * jnp.exp(-(ratio * ratio)) * live
            for d in range(3):
                force[d, i, g] = force[d, i, g] * strength
        return carry

    lax.fori_loop(0, edge, push, 0, unroll=8)


class Grid:
    def __init__(self, xs, ys, lanes):
        self.xs, self.ys, self.lanes = xs, ys, lanes
        self.here = pl.ds(SUB, ys)
        self.below = pl.ds(SUB - 1, ys)
        self.above = pl.ds(SUB + 1, ys)
        self.rows = ys + 2 * SUB
        self.shape = (3, xs + 2, self.rows, lanes)
        self.lane = iota((ys, lanes), 1)

    def row_of(self, ref, c, x, row):
        flat = ref.reshape(3 * (self.xs + 2) * self.rows, self.lanes)
        return flat.at[pl.ds((c * (self.xs + 2) + x) * self.rows + row, SUB, stride=self.rows), :]

    def fill_rows(self, ref, low, high):
        for c in range(3):
            for x in range(0, self.xs, SUB):
                part = pl.ds(x, SUB)
                self.row_of(ref, c, x + 1, SUB - 1)[...] = low[c, part]
                self.row_of(ref, c, x + 1, SUB + self.ys)[...] = high[c, part]

    def take_rows(self, ref, ysend):
        for c in range(3):
            for x in range(0, self.xs, SUB):
                part = pl.ds(x, SUB)
                ysend[0, c, part] = self.row_of(ref, c, x + 1, SUB + self.ys - 1)[...]
                ysend[1, c, part] = self.row_of(ref, c, x + 1, SUB)[...]

    def combine(self, zlow, zhigh, comb):
        high = pltpu.roll(zhigh[...], self.lanes - 2, 1)
        for c in range(3):
            comb[c] = jnp.where(self.lane % 4 == c, zlow[...], high)

    def pack(self, value, c, x, faces):
        lane = self.lane[: value.shape[0]] - 4 * x
        turned = pltpu.roll(value, 4 * x + c + 1, 1)
        return jnp.where(lane == c, turned, faces[0]), jnp.where(lane == c + 1, turned, faces[1])

    def shift(self, src, shifts, near, pieces, also):
        span = self.xs // pieces

        def part(t, carry):
            left = [halves(src[c, 1 + span * t + n, self.here]) for c in range(3) for n in range(span)]
            both = jnp.dot(jnp.concatenate(left, axis=0), shifts[...], preferred_element_type=f32)
            for c in range(3):
                for n in range(span):
                    at = (c * span + n) * self.ys
                    for e in range(2):
                        near[c, span * t + n, e] = both[at : at + self.ys, e * self.lanes : (e + 1) * self.lanes]
            also(t)
            return carry

        lax.fori_loop(0, pieces, part, 0)

    def section(self, src, comb, near, scale, emit, ends_done, unroll):
        h = scale * grid_step * viscosity
        lane = self.lane[:SUB]
        first, last = lane == 0, lane == self.lanes - 1

        def plane(x, carry):
            for y in range(0, self.ys, SUB):
                rows, tile = pl.ds(SUB + y, SUB), pl.ds(y, SUB)
                centre = [src[c, x + 1, rows] for c in range(3)]
                w = [(0.5 * scale * grid_step) * v for v in centre]
                up, down = [h - v for v in w], [h + v for v in w]
                rim = jnp.where(first, down[2], jnp.where(last, up[2], 0.0))
                values = []
                for c in range(3):
                    turn = lax.rem(2 * self.lanes - c - 4 * x, self.lanes)
                    halo = pltpu.roll(comb[c, tile], turn, 1)
                    values.append(
                        (scale - 6.0 * h) * centre[c]
                        + up[0] * src[c, x + 2, rows]
                        + down[0] * src[c, x, rows]
                        + up[1] * src[c, x + 1, pl.ds(SUB + y + 1, SUB)]
                        + down[1] * src[c, x + 1, pl.ds(SUB + y - 1, SUB)]
                        + up[2] * near[c, x, 1, tile]
                        + down[2] * near[c, x, 0, tile]
                        + rim * halo
                    )
                emit(x, y, values)
            return carry

        if ends_done is None:
            lax.fori_loop(0, self.xs, plane, 0, unroll=unroll)
            return
        plane(0, 0)
        plane(self.xs - 1, 0)
        ends_done()
        lax.fori_loop(1, self.xs - 1, plane, 0, unroll=unroll)


def step_kernel(
    sizes, corners, owners, v_hbm, lev_hbm,
    vel, pred, near1, yrecv1, zrecv1, force, native_a, native_b,
    yrecv0, zrecv0, ysend, zsend, comb, near0, shifts, windows, wide,
    native, lev, mi, di, mj, dj, mot, psa, psb, sign, rate,
    local_sem, lev_sem, send_sem, recv_sem,
):
    _, xs, ys, lanes = v_hbm.shape
    grid = Grid(xs, ys, lanes)
    slots = corners.shape[1]
    edge = lev.shape[0]
    box = Box(edge, lanes, slots)
    inner = pl.ds(1, xs)
    loads = [
        pltpu.make_async_copy(v_hbm.at[c], vel.at[c, inner, grid.here], local_sem.at[c]) for c in range(3)
    ]
    levels = [
        pltpu.make_async_copy(lev_hbm.at[:, pl.ds(h * lanes, lanes)], native.at[h], lev_sem.at[h])
        for h in range(box.halves)
    ]
    for part in loads + levels:
        part.start()
    ups, downs = [], []
    for axis in ("gx", "gy", "gz"):
        me, n = lax.axis_index(axis), sizes[axis]
        ups.append({axis: lax.rem(me + 1, n)})
        downs.append({axis: lax.rem(me + n - 1, n)})
    barrier = pltpu.get_barrier_semaphore()
    for target in ups + downs:
        pl.semaphore_signal(barrier, inc=1, device_id=target, device_id_type=MESH)
    shifts[...] = shift_matrix(lanes)
    windows[...] = window_matrix(box, corners)

    def exchange(r, src, yrecv, zrecv):
        def copy(n, src, dst, target):
            return pltpu.make_async_remote_copy(
                src_ref=src,
                dst_ref=dst,
                send_sem=send_sem.at[r, n],
                recv_sem=recv_sem.at[r, n],
                device_id=target,
                device_id_type=MESH,
            )

        return [
            copy(0, src.at[:, xs, grid.here], src.at[:, 0, grid.here], ups[0]),
            copy(1, src.at[:, 1, grid.here], src.at[:, xs + 1, grid.here], downs[0]),
            copy(2, ysend.at[r, 0], yrecv.at[0], ups[1]),
            copy(3, ysend.at[r, 1], yrecv.at[1], downs[1]),
            copy(4, zsend.at[r, 0], zrecv.at[0], ups[2]),
            copy(5, zsend.at[r, 1], zrecv.at[1], downs[2]),
        ]

    copies = exchange(0, vel, yrecv0, zrecv0), exchange(1, pred, yrecv1, zrecv1)

    at = [lax.axis_index(axis) for axis in ("gx", "gy", "gz")]
    low = at[2] == 0
    first_in = jnp.logical_and(low, jnp.logical_and(at[0] == 0, at[1] < 2))

    def send_blocks(when):
        @pl.when(when)
        def _():
            pl.semaphore_wait(barrier, 6)
            for copy in copies[0][4:] + copies[0][:4]:
                copy.start()

    blank = jnp.zeros((ys, lanes), f32)
    faces = blank, blank
    for c in range(3):
        loads[c].wait()

        def pack(x, faces, c=c):
            return grid.pack(vel[c, x + 1, grid.here], c, x, faces)

        faces = lax.fori_loop(0, xs, pack, faces, unroll=True)
    zsend[0, 0], zsend[0, 1] = faces
    zsend[1, 0], zsend[1, 1] = blank, blank
    grid.take_rows(vel, ysend.at[0])
    send_blocks(jnp.logical_not(first_in))
    for part in levels:
        part.wait()
    span = xs // 2

    def spread(t, carry):
        left = [halves(vel[c, span * t + n + 1, grid.here]) for c in range(3) for n in range(span)]
        both = jnp.dot(jnp.concatenate(left, axis=0), windows[...], preferred_element_type=f32)
        for c in range(3):
            for n in range(span):
                at = (c * span + n) * ys
                for g in range(box.groups):
                    wide[c, g, span * t + n] = both[at : at + ys, g * lanes : (g + 1) * lanes]
        fetch_levels(box, native, lev, t * (edge // 2), edge // 2)
        return carry

    lax.fori_loop(0, 2, spread, 0)
    gather = gather_motion(box, corners, wide, mot)
    grid.shift(vel, shifts, near0, 2, lambda t: gather(t * (edge // 2), edge // 2))
    send_blocks(first_in)
    advect_levels(box, lev, mi, di, mj, dj, mot, psa, sign, rate)
    two_sweeps = reinitialize(box, psa, psb, sign, rate)
    ahead = jnp.where(first_in, AHEAD[2], jnp.where(low, AHEAD[1], AHEAD[0]))
    two_sweeps(ahead)
    for copy in copies[0]:
        copy.wait()
    grid.fill_rows(vel, yrecv0.at[0], yrecv0.at[1])
    grid.combine(zrecv0.at[0], zrecv0.at[1], comb)

    def first(x, y, values):
        tile = pl.ds(y, SUB)
        faces = zsend[1, 0, tile], zsend[1, 1, tile]
        for c, value in enumerate(values):
            pred[c, x + 1, pl.ds(SUB + y, SUB)] = value
            faces = grid.pack(value, c, x, faces)
        zsend[1, 0, tile], zsend[1, 1, tile] = faces

    grid.section(vel, comb, near0, 1.0, first, lambda: [copy.start() for copy in copies[1][:2]], PLANES)
    for copy in copies[1][4:]:
        copy.start()
    grid.take_rows(pred, ysend.at[1])
    for copy in copies[1][2:4]:
        copy.start()
    grid.shift(pred, shifts, near1, FUSE, lambda t: two_sweeps(1))
    two_sweeps(ITERS // 2 - FUSE - ahead)
    curve_levels(box, owners, psa, mi, mj, di, force, native_a, native_b)
    for copy in copies[1]:
        copy.wait()


def kept(x):
    return pltpu.with_memory_space_constraint(x, pltpu.HBM)


def step_call(velocity, box_level, corners, owner_list):
    sizes = {axis: lax.axis_size(axis) for axis in ("gx", "gy", "gz")}
    _, xs, ys, lanes = velocity.shape
    slots, edge, plane = box_level.shape
    groups = slots * edge // lanes
    vmem = pltpu.VMEM
    grid_shape = (3, xs + 2, ys + 2 * SUB, lanes)
    tall = (edge, groups, edge + 2 * SUB, lanes)
    flat = (edge, groups, edge, lanes)
    native = (plane // lanes, slots * edge, lanes)
    smem = pl.BlockSpec(memory_space=pltpu.SMEM)
    return pl.pallas_call(
        functools.partial(step_kernel, sizes),
        out_shape=(
            vmem(grid_shape, f32),
            vmem(grid_shape, f32),
            vmem((3, xs, 2, ys, lanes), f32),
            vmem((2, 3, xs, lanes), f32),
            vmem((2, ys, lanes), f32),
            vmem((3,) + flat, f32),
            vmem(native, f32),
            vmem(native, f32),
        ),
        in_specs=[smem, smem, pl.BlockSpec(memory_space=pltpu.HBM), pl.BlockSpec(memory_space=pltpu.HBM)],
        out_specs=(pl.BlockSpec(memory_space=vmem),) * 8,
        scratch_shapes=[
            vmem((2, 3, xs, lanes), f32),
            vmem((2, ys, lanes), f32),
            vmem((2, 2, 3, xs, lanes), f32),
            vmem((2, 2, ys, lanes), f32),
            vmem((3, ys, lanes), f32),
            vmem((3, xs, 2, ys, lanes), f32),
            vmem((2 * lanes, 2 * lanes), bf16),
            vmem((2 * lanes, groups * lanes), bf16),
            vmem((3, groups, xs, ys, lanes), f32),
            vmem(native, f32),
            vmem(tall, f32),
            vmem((edge + 1,) + flat[1:], f32),
            vmem((edge + 4,) + flat[1:], f32),
            vmem(tall, f32),
            vmem(tall, f32),
            vmem((3,) + flat, f32),
            vmem(tall, f32),
            vmem(tall, f32),
            vmem(flat, f32),
            vmem(flat, f32),
            pltpu.SemaphoreType.DMA((3,)),
            pltpu.SemaphoreType.DMA((plane // lanes,)),
            pltpu.SemaphoreType.DMA((2, 6)),
            pltpu.SemaphoreType.DMA((2, 6)),
        ],
        compiler_params=pltpu.CompilerParams(
            collective_id=0, has_side_effects=True, vmem_limit_bytes=36 * MIB
        ),
    )(corners, owner_list, kept(velocity), kept(box_level.reshape(slots * edge, plane)))


def force_kernel(
    corners, vel, pred, near, yrecv, zrecv, force, native_a, native_b,
    o_hbm, set_hbm, ben_hbm,
    o_ref, comb, place, out_sem, small_sem,
):
    _, xs, ys, lanes = o_ref.shape
    grid = Grid(xs, ys, lanes)
    slots = corners.shape[1]
    edge = force.shape[1]
    box = Box(edge, lanes, slots)
    per = box.per
    stores = []
    for h in range(box.halves):
        part_h = pl.ds(h * lanes, lanes)
        stores.append(pltpu.make_async_copy(native_a.at[h], set_hbm.at[:, part_h], small_sem.at[0, h]))
        stores.append(pltpu.make_async_copy(native_b.at[h], ben_hbm.at[:, part_h], small_sem.at[1, h]))
    for copy in stores:
        copy.start()
    grid.combine(zrecv.at[0], zrecv.at[1], comb)

    def second(x, y, values):
        for c, value in enumerate(values):
            o_ref[c, x, pl.ds(y, SUB)] = 0.5 * vel[c, x + 1, pl.ds(SUB + y, SUB)] + value

    grid.fill_rows(pred, yrecv.at[0], yrecv.at[1])
    grid.section(pred, comb, near, 0.5, second, None, 8)

    wide = iota((edge, lanes), 1)

    offset = iota((edge, lanes), 1) - iota((edge, lanes), 0)
    spots = [(c, i) for c in range(3) for i in range(edge)]

    def turned(n, force_at):
        ax, ay, az = corners[0, n], corners[1, n], corners[2, n]
        turn = lax.rem(az + lanes - n % per * edge, lanes)
        inside = jnp.logical_and(wide >= az, wide < az + edge)
        for at in range(0, len(spots), TURN):
            some = spots[at : at + TURN]
            blocks = [pltpu.roll(force_at(c, i), turn, 1) for c, i in some]
            olds = [o_ref[c, ax + i, pl.ds(ay, edge), :] for c, i in some]
            for (c, i), old, block in zip(some, olds, blocks):
                o_ref[c, ax + i, pl.ds(ay, edge), :] = old + jnp.where(inside, block, 0.0)

    def deposit(t, carry):
        base = t * DEPOSIT
        g = base // per

        def force_at(c, i):
            return force[c, i, g]

        for e in range(2):
            slot = base + e
            mark = ones(offset == corners[2, slot])
            blank = jnp.zeros_like(mark)
            for r in range(per):
                value = jnp.where(slot % per == r, mark, blank)
                for part in range(2):
                    place[pl.ds(part * lanes + r * edge, edge), e * lanes : (e + 1) * lanes] = value
        left = jnp.concatenate([halves(force_at(c, i)) for c, i in spots], axis=0)
        both = jnp.dot(left, place[...], preferred_element_type=f32)
        for e in range(2, DEPOSIT):
            turned(base + e, force_at)
        for e in range(2):
            ax, ay = corners[0, base + e], corners[1, base + e]
            for n, (c, i) in enumerate(spots):
                rows = pl.ds(ay, edge)
                o_ref[c, ax + i, rows, :] = (
                    o_ref[c, ax + i, rows, :]
                    + both[n * edge : (n + 1) * edge, e * lanes : (e + 1) * lanes]
                )
        return carry

    lax.fori_loop(0, slots // DEPOSIT, deposit, 0)
    for c in range(3):
        stores.append(pltpu.make_async_copy(o_ref.at[c], o_hbm.at[c], out_sem.at[c]))
        stores[-1].start()
    for copy in stores:
        copy.wait()


def force_call(shapes, block, corners, handed):
    slots, edge, plane = shapes
    _, xs, ys, lanes = block
    flat = (slots * edge, plane)
    whole = pl.BlockSpec(memory_space=pltpu.VMEM)
    smem = pl.BlockSpec(memory_space=pltpu.SMEM)
    handed = [pltpu.with_memory_space_constraint(a, pltpu.VMEM) for a in handed]
    result, settled, bending = pl.pallas_call(
        force_kernel,
        out_shape=(
            jax.ShapeDtypeStruct(block, f32),
            jax.ShapeDtypeStruct(flat, f32),
            jax.ShapeDtypeStruct(flat, f32),
        ),
        in_specs=[smem] + [whole] * 8,
        out_specs=(pl.BlockSpec(memory_space=pltpu.HBM),) * 3,
        scratch_shapes=[
            pltpu.VMEM(block, f32),
            pltpu.VMEM((3, ys, lanes), f32),
            pltpu.VMEM((2 * lanes, 2 * lanes), bf16),
            pltpu.SemaphoreType.DMA((3,)),
            pltpu.SemaphoreType.DMA((2, plane // lanes)),
        ],
        compiler_params=pltpu.CompilerParams(vmem_limit_bytes=24 * MIB),
    )(corners, *handed)
    return result, settled.reshape(shapes), bending.reshape(shapes)


def local(velocity, box_level, corners, owner_list):
    turned, owner_list = kept(corners.T), kept(owner_list)
    handed = step_call(velocity, box_level, turned, owner_list)
    return force_call(box_level.shape, velocity.shape, turned, handed)


def solution(mesh):
    placed = (
        P(None, "gx", "gy", "gz"),
        P(("gx", "gy", "gz"), None, None),
        P(("gx", "gy", "gz"), None),
        P(("gx", "gy", "gz")),
    )
    return jax.shard_map(
        local,
        mesh=mesh,
        in_specs=placed,
        out_specs=(
            P(None, "gx", "gy", "gz"),
            P(("gx", "gy", "gz"), None, None),
            P(("gx", "gy", "gz"), None, None),
        ),
        check_vma=False,
    )
```
